256 devices in a mesh: bead: 32 (over x, z_lo, core), space: 8 (over y, z_hi).
Axes of the slice: x: 4, y: 4, z: 8 (z_hi: 2, z_lo: 4; z = z_hi * 4 + z_lo), core: 2. Of those that a mesh axis runs over, the one named last changes fastest.
Arguments:
- positions: float32 [32, 3, 4096], P('bead', None, 'space'), may hold values from -6 to 6
- momenta: float32 [32, 3, 4096], P('bead', None, 'space'), may hold values from -6 to 6
- species: int32 [4096], P('space'), may hold values from 0 to 1
- neighbours: int32 [8, 4096], P(None, 'space'), may hold values from 0 to 1023
- send_list: int32 [4096], P('space'), may hold values from 0 to 511
- embedding: float32 [2, 128], replicated, may hold values from -4 to 4
- radial_one: float32 [8, 128], replicated, may hold values from -4 to 4
- radial_two: float32 [8, 128], replicated, may hold values from -4 to 4
- mix_one: float32 [128, 384], replicated, may hold values from -0.3125 to 0.3125
- mix_two: float32 [128, 384], replicated, may hold values from -0.3125 to 0.3125
- read_one: float32 [128], replicated, may hold values from -0.5 to 0.5
- read_two: float32 [128], replicated, may hold values from -0.5 to 0.5
Outputs:
- new_positions: float32 [32, 3, 4096], P('bead', None, 'space')
- new_momenta: float32 [32, 3, 4096], P('bead', None, 'space')
The draws below stay inside these ranges and needn't reach their ends.
Inputs may be any that keep to these rules, and one draw needn't show every extreme that they name: `neighbours`: positions in the extended set of the atom's own domain: below 256 the ghosts from the lower domain, then the 512 own atoms, then the ghosts from the upper domain. `send_list`: entries d * 512 to d * 512 + 255 are sent to domain d - 1, the next 256 to domain d + 1.
All inputs are finite; a program needn't handle non-finite values.
Results may differ from the reference program's by a relative error of at most 0.0003.
Values sent between devices are 32-bit elements; how exact they have to be, the bound alone decides.
A program may use at most 128 MiB of HBM per device.

```python
import math
import jax
import jax.numpy as jnp
from jax import lax

C = 128
NB = 8
K = 8
ATOMS_DEV = 512
ATOMS = 4096
BEADS = 32
N_SPACE = 8


def plant(values, key, least, high):
    shape = values.shape
    index_at = [jax.random.randint(jax.random.fold_in(key, axis), (), 0, shape[axis]) for axis in range(len(shape))]
    values = values.at[tuple(index_at)].set(least)
    longest = shape.index(max(shape))
    index_at[longest] = (index_at[longest] + 1) % shape[longest]
    return values.at[tuple(index_at)].set(high)


def shard_levels(key, extent, shards, smallest, top_value):
    loudness = 1.0
    for position, shards_of in shards:
        draws = jax.random.uniform(jax.random.fold_in(jax.random.fold_in(key, 6), position), (shards_of,), jnp.float32, smallest / len(shards), top_value / len(shards))
        loudness = loudness * jnp.repeat(jnp.exp(draws), extent[position] // shards_of).reshape((-1,) + (1,) * (len(extent) - 1 - position))
    return loudness


def gaussian(key, extent, deviation, most, cuts=(), held_as=jnp.bfloat16):
    array = jax.random.normal(key, extent, jnp.float32) * deviation
    if len(cuts) > 0:
        array = shard_levels(key, extent, cuts, -0.22, 0.18) * array
    return jnp.clip(array, min=-most, max=most).astype(held_as)


def setup_inputs(seed: int = 0) -> dict:
    arg_keys = jax.random.split(jax.random.key(seed), 13)
    positions = gaussian(arg_keys[0], (BEADS, 3, ATOMS), 1.5, 6.0, ((0, 32), (2, 8)), jnp.float32)
    momenta = gaussian(arg_keys[1], (BEADS, 3, ATOMS), 1.0, 6.0, ((0, 32), (2, 8)), jnp.float32)
    species = plant(jax.random.randint(arg_keys[2], (ATOMS,), 0, 2), jax.random.fold_in(arg_keys[2], 1), 0, 1).astype(jnp.int32)
    neighbours = plant(jax.random.randint(arg_keys[3], (K, ATOMS), 0, 2 * ATOMS_DEV), jax.random.fold_in(arg_keys[3], 1), 0, (2 * ATOMS_DEV) - 1).astype(jnp.int32)
    send_list = plant(jax.random.randint(arg_keys[4], (ATOMS,), 0, ATOMS_DEV), jax.random.fold_in(arg_keys[4], 1), 0, ATOMS_DEV - 1).astype(jnp.int32)
    embedding = gaussian(arg_keys[5], (2, C), 1.0, 4.0, (), jnp.float32)
    radial_one = gaussian(arg_keys[6], (NB, C), 1.0, 4.0, (), jnp.float32)
    radial_two = gaussian(arg_keys[7], (NB, C), 1.0, 4.0, (), jnp.float32)
    mix_one = gaussian(arg_keys[8], (C, 3 * C), (3 * C) ** -0.5, 0.3125, (), jnp.float32)
    mix_two = gaussian(arg_keys[9], (C, 3 * C), (3 * C) ** -0.5, 0.3125, (), jnp.float32)
    read_one = gaussian(arg_keys[10], (C,), C ** -0.5, 0.5, (), jnp.float32)
    read_two = gaussian(arg_keys[11], (C,), C ** -0.5, 0.5, (), jnp.float32)
    return dict(positions=positions, momenta=momenta, species=species, neighbours=neighbours, send_list=send_list, embedding=embedding, radial_one=radial_one, radial_two=radial_two, mix_one=mix_one, mix_two=mix_two, read_one=read_one, read_two=read_two)


EXACT = lax.Precision.HIGHEST
STEP = 2.0
HALF_STEP = 1.0
HEAVY = 16.0
SQRT3 = math.sqrt(3.0)
SQRT5 = math.sqrt(5.0)
SQRT15 = math.sqrt(15.0)

def harmonics(unit):
    ux, uy, uz = (unit[0], unit[1], unit[2])
    return jnp.stack([jnp.ones_like(ux), SQRT3 * ux, SQRT3 * uy, SQRT3 * uz, SQRT15 * ux * uy, SQRT15 * uy * uz, 0.5 * SQRT5 * (2.0 * uz * uz - ux * ux - uy * uy), SQRT15 * ux * uz, 0.5 * SQRT15 * (ux * ux - uy * uy)])

def interaction(ext_coords, centre, slots, ext_feat, radial, mixing):
    neigh_count = slots.shape[0]
    atom_count = slots.shape[1]
    flat_slots = slots.reshape(-1)
    relative = jnp.take(ext_coords, flat_slots, axis=1).reshape(3, neigh_count, atom_count) - centre[:, None, :]
    soft_dist = jnp.sqrt(lax.optimization_barrier(jnp.sum(relative * relative, axis=0)) + 1.0)
    sphere = harmonics(relative / soft_dist)
    centres = 1.0 + jnp.arange(radial.shape[0]).astype(jnp.float32)
    basis = jnp.exp(-0.5 * (soft_dist[None] - centres[:, None, None]) ** 2)
    edge_weight = jnp.einsum('nc,nka->cka', radial, basis, precision=EXACT)
    carried = edge_weight * jnp.take(ext_feat, flat_slots, axis=1).reshape(-1, neigh_count, atom_count)
    moments = jnp.einsum('lka,cka->lca', sphere, carried, precision=EXACT) / neigh_count
    squares = moments * moments
    invariants = jnp.concatenate([squares[0], lax.optimization_barrier(jnp.sum(squares[1:4], axis=0)), lax.optimization_barrier(jnp.sum(squares[4:9], axis=0))], axis=0)
    return jnp.dot(mixing, invariants, precision=EXACT)

def embed(embedding, flags):
    return embedding[0][:, None] + flags[None, :] * (embedding[1] - embedding[0])[:, None]

def normal_modes(bead_total):
    bead_idx = jnp.arange(bead_total).astype(jnp.float32)[:, None]
    mode_idx = jnp.arange(bead_total).astype(jnp.float32)[None, :]
    phase = 2.0 * jnp.pi * bead_idx * mode_idx / bead_total
    half_total = bead_total // 2
    table = jnp.where(mode_idx < half_total, math.sqrt(2.0 / bead_total) * jnp.cos(phase), math.sqrt(2.0 / bead_total) * jnp.sin(phase))
    table = jnp.where(mode_idx == half_total, jnp.cos(jnp.pi * bead_idx) / math.sqrt(bead_total), table)
    table = jnp.where(mode_idx == 0, 1.0 / math.sqrt(bead_total), table)
    return table

def mode_factors(bead_total):
    mode_idx = jnp.arange(bead_total).astype(jnp.float32)
    angles = float(bead_total) * jnp.sin(jnp.pi * mode_idx / bead_total)
    safe_angles = jnp.where(mode_idx == 0, 1.0, angles)
    cosine = jnp.cos(angles)
    reach = jnp.where(mode_idx == 0, STEP, STEP * jnp.sin(angles) / safe_angles)
    stiff = angles * jnp.sin(angles) / STEP
    return (cosine, reach, stiff)

def reference(positions, momenta, species, neighbours, send_list, embedding, radial_one, radial_two, mix_one, mix_two, read_one, read_two):
    domains = N_SPACE
    per_domain = ATOMS_DEV
    ghost_rows = per_domain // 2
    neigh_count = neighbours.shape[0]
    sends = send_list.reshape(domains, per_domain)
    offsets = (jnp.arange(domains).astype(jnp.int32) * per_domain)[:, None]
    lower_ids = jnp.roll(offsets, 1, axis=0) + jnp.roll(sends, 1, axis=0)[:, ghost_rows:]
    own_ids = offsets + jnp.arange(per_domain).astype(jnp.int32)[None, :]
    upper_ids = jnp.roll(offsets, -1, axis=0) + jnp.roll(sends, -1, axis=0)[:, :ghost_rows]
    extended = jnp.concatenate([lower_ids, own_ids, upper_ids], axis=1).astype(jnp.int32)
    local_ids = neighbours.reshape(neigh_count, domains, per_domain)
    wide_ext = jnp.broadcast_to(extended[None], (neigh_count, domains, 2 * per_domain))
    global_ids = jnp.take_along_axis(wide_ext, local_ids, axis=2).reshape(neigh_count, domains * per_domain).astype(jnp.int32)
    flags = species.astype(jnp.float32)
    masses = HEAVY - (HEAVY - 1.0) * flags
    base_feat = embed(embedding, flags)

    def energy(coords):
        hidden = base_feat + jax.nn.silu(interaction(coords, coords, global_ids, base_feat, radial_one, mix_one))
        top = interaction(coords, coords, global_ids, hidden, radial_two, mix_two)
        return jnp.sum(jnp.dot(read_two, jax.nn.silu(top), precision=EXACT)) + jnp.sum(jnp.dot(read_one, hidden, precision=EXACT))

    def bead_force(coords):
        return -jax.grad(energy)(coords)
    forces = lax.map(bead_force, positions)
    kicked = momenta + HALF_STEP * forces
    bead_total = positions.shape[0]
    modes_mat = normal_modes(bead_total)
    cosine, reach, stiff = mode_factors(bead_total)
    mode_q = jnp.einsum('bk,bca->kca', modes_mat, positions, precision=EXACT)
    mode_p = jnp.einsum('bk,bca->kca', modes_mat, kicked, precision=EXACT)
    moved_q = cosine[:, None, None] * mode_q + reach[:, None, None] * mode_p / masses[None, None, :]
    moved_p = cosine[:, None, None] * mode_p - stiff[:, None, None] * masses[None, None, :] * mode_q
    new_positions = jnp.einsum('bk,kca->bca', modes_mat, moved_q, precision=EXACT)
    new_momenta = jnp.einsum('bk,kca->bca', modes_mat, moved_p, precision=EXACT)
    return (new_positions, new_momenta)
```

```python
import math

import numpy as np

import jax
import jax.numpy as jnp
from jax import lax
from jax.experimental import pallas as pl
from jax.experimental.pallas import tpu as pltpu
from jax.sharding import PartitionSpec as P

STEP = 2.0
HEAVY = 16.0
SQRT3 = math.sqrt(3.0)
SQRT5 = math.sqrt(5.0)
SQRT15 = math.sqrt(15.0)
F32 = jnp.float32
BF16 = jnp.bfloat16
I32 = jnp.int32
NT = (((1,), (1,)), ((), ()))
VM = pl.BlockSpec(memory_space=pltpu.VMEM)
SM = pl.BlockSpec(memory_space=pltpu.SMEM)
MESH = pl.DeviceIdType.MESH


def dot(a, b):
    return jnp.dot(a, b, preferred_element_type=F32)


def dot_nt(a, b):
    return lax.dot_general(a, b, NT, preferred_element_type=F32)


def split(x):
    hi = x.astype(BF16)
    return hi, (x - hi.astype(F32)).astype(BF16)


def halves(x):
    n = x.shape[0] // 2
    return x[:n] + x[n:]


def lane_take(tiles, idx):
    low = idx & 127
    high = idx >> 7
    out = jnp.take_along_axis(tiles[0], low, axis=1)
    for t in range(1, len(tiles)):
        out = jnp.where(high == t, jnp.take_along_axis(tiles[t], low, axis=1), out)
    return out


def spread(row, count=8):
    return jnp.broadcast_to(row, (count, row.shape[1]))


def tiles_of(ref, first):
    return [ref[first : first + 8, t * 128 : (t + 1) * 128] for t in range(4)]


def compute_kernel(
    own, low1, up1, low2, up2, emb, r1, r2, mix1, mix2, rd1, rd2,
    to_low, to_up, to_low2, to_up2, kept,
    nb_s, geo, yy, bb, hot, m1, hs, ds1, gg, ww, m2, dg, dw, part, two, dh, dr, fl,
):
    def send_of(ref):
        return ref[4:5, :].astype(I32)

    sends = [send_of(r) for r in (own, low1, up1, low2, up2)]

    def slots(ref, send, half, first=0):
        tiles = tiles_of(ref, first)
        out = []
        for t in range(2):
            at = half * 256 + t * 128
            out.append(lane_take(tiles, spread(send[:, at : at + 128])))
        return out

    own_t = tiles_of(own, 0)
    ext_own = slots(low1, sends[1], 1) + own_t + slots(up1, sends[2], 0)
    ext_low = slots(low2, sends[3], 1) + tiles_of(low1, 0) + slots(own, sends[0], 0)
    ext_up = slots(own, sends[0], 1) + tiles_of(up1, 0) + slots(up2, sends[4], 0)
    nb_t = slots(low1, sends[1], 1, 8) + tiles_of(own, 8) + slots(up1, sends[2], 0, 8)
    nb_t = [x.astype(I32) for x in nb_t]

    for e in range(8):
        cols = slice(e * 128, (e + 1) * 128)
        ext = ext_low if e < 2 else (ext_own if e < 6 else ext_up)
        idx = nb_t[e]
        nb_s[:, cols] = idx
        fl[:, cols] = spread(ext_own[e][3:4])
        got = [lane_take([spread(x[c : c + 1]) for x in ext], idx) for c in range(4)]
        rx, ry, rz = [got[c] - spread(ext_own[e][c : c + 1]) for c in range(3)]
        s = jnp.sqrt(rx * rx + ry * ry + rz * rz + 1.0)
        inv = 1.0 / s
        ux, uy, uz = rx * inv, ry * inv, rz * inv
        for c, v in enumerate((ux, uy, uz, s, inv, got[3])):
            geo[c, :, cols] = v
        ys = (
            SQRT3 * ux, SQRT3 * uy, SQRT3 * uz,
            SQRT15 * ux * uy, SQRT15 * uy * uz,
            0.5 * SQRT5 * (2.0 * uz * uz - ux * ux - uy * uy),
            SQRT15 * ux * uz, 0.5 * SQRT15 * (ux * ux - uy * uy),
        )
        for l in range(8):
            yy[l, :, cols] = ys[l]
        for n in range(8):
            bb[n, :, cols] = jnp.exp(-0.5 * (s - (1.0 + n)) ** 2)

    @pl.loop(0, 8)
    def _(rc):
        at = pl.multiple_of(rc * 128, 128)
        ids = lax.broadcasted_iota(I32, (128, 512), 0) + at
        for k in range(8):
            row = jnp.broadcast_to(nb_s[k : k + 1, 256:768], (128, 512))
            hot[pl.ds(at, 128), k * 512 : (k + 1) * 512] = jnp.where(ids == row, 1.0, 0.0).astype(BF16)

    w_rows = []
    for f in range(2):
        for n in range(8):
            w_rows.append(spread(r1[n : n + 1, :] * emb[f : f + 1, :] * 0.125))
    wt = jnp.concatenate(w_rows, axis=0)
    wth, wtl = split(wt)
    wh, wl = split(jnp.transpose(wt))
    zero = jnp.zeros((128, 128), BF16)
    wf = jnp.concatenate([jnp.concatenate([wh, wh], 1), jnp.concatenate([wl, zero], 1)], 0)
    wtf = jnp.concatenate([jnp.concatenate([wth, wth], 1), jnp.concatenate([wtl, zero], 1)], 0)
    r2s = r2[...] * 0.125
    rows = jnp.concatenate([emb[...], rd1[...], rd2[...], jnp.zeros((4, 128), F32), r2s], 0)
    colmat = jnp.transpose(jnp.concatenate([rows, jnp.zeros((112, 128), F32)], 0))
    e0, e1 = colmat[:, 0:1], colmat[:, 1:2]
    c_rd1, c_rd2 = colmat[:, 2:3], colmat[:, 3:4]
    m1h, m1l = split(mix1[...])
    m1s = jnp.concatenate([m1h, m1l], 0)
    m1t = jnp.transpose(mix1[...])
    m1th, m1tl = split(m1t)
    m1ts = jnp.concatenate([m1th, m1tl], 0)
    m2h, m2l = split(mix2[...])
    m2s = jnp.concatenate([m2h, m2l], 0)
    m2th, m2tl = split(jnp.transpose(mix2[...]))
    m2ts = jnp.concatenate([m2th, m2tl], 0)

    def mixed(ws, wh_, x):
        hi, lo = split(x)
        return halves(dot(ws, hi)) + dot(wh_, lo)

    @pl.loop(0, 4)
    def _(ch):
        sl = pl.ds(pl.multiple_of(ch * 256, 256), 256)
        f = geo[5, :, sl]
        bs = []
        for n in range(8):
            bs.append(bb[n, :, sl] * (1.0 - f))
        for n in range(8):
            bs.append(bb[n, :, sl] * f)
        q = [None, None, None]
        for l in range(9):
            z = jnp.concatenate(bs if l == 0 else [yy[l - 1, :, sl] * b for b in bs], 0)
            m = halves(dot(wf, jnp.concatenate(split(z), 0)))
            m1[l, :, sl] = m
            g = 0 if l == 0 else (1 if l < 4 else 2)
            q[g] = m * m if q[g] is None else q[g] + m * m
        v = mixed(m1s, m1h, jnp.concatenate(q, 0))
        sg = 1.0 / (1.0 + jnp.exp(-v))
        fc = fl[0:1, sl]
        h = e0 + fc * (e1 - e0) + v * sg
        ds1[:, sl] = sg * (1.0 + v * (1.0 - sg))
        hs[:, sl] = jnp.concatenate(split(h), 0)

    own_lanes = slice(256, 768)
    iota8 = lax.broadcasted_iota(I32, (8, 512), 0).astype(F32)
    r2th, r2tl = split(colmat[:, 8:16])
    r2lhs = jnp.concatenate([r2th.astype(F32), r2th.astype(F32), r2tl.astype(F32)], 1).astype(BF16)

    def basis(k):
        off = spread(geo[3, k : k + 1, own_lanes]) - 1.0 - iota8
        return off, jnp.exp(-0.5 * off * off)

    for k in range(8):
        gg[k] = halves(dot(hs[...], hot[:, k * 512 : (k + 1) * 512]))
        _, bk = basis(k)
        bh, bl = split(bk)
        rhs = jnp.concatenate([bh.astype(F32), bl.astype(F32), bh.astype(F32)], 0).astype(BF16)
        ww[k] = dot(r2lhs, rhs)

    def y_row(l, k, it):
        at = pl.multiple_of(256 + it * 128, 128)
        return yy[l - 1, k : k + 1, pl.ds(at, 128)]

    @pl.loop(0, 16)
    def _(step):
        it = step // 4
        rows_ = pl.ds(pl.multiple_of((step % 4) * 32, 32), 32)
        lanes = pl.ds(pl.multiple_of(it * 128, 128), 128)
        car = [gg[k, rows_, lanes] * ww[k, rows_, lanes] for k in range(8)]
        acc = car[0]
        for k in range(1, 8):
            acc = acc + car[k]
        m2[0, rows_, lanes] = acc
        for l in range(1, 9):
            acc = y_row(l, 0, it) * car[0]
            for k in range(1, 8):
                acc = acc + y_row(l, k, it) * car[k]
            m2[l, rows_, lanes] = acc

    @pl.loop(0, 2)
    def _(ch):
        sl = pl.ds(pl.multiple_of(ch * 256, 256), 256)
        q = [None, None, None]
        for l in range(9):
            m = m2[l, :, sl]
            g = 0 if l == 0 else (1 if l < 4 else 2)
            q[g] = m * m if q[g] is None else q[g] + m * m
        v = mixed(m2s, m2h, jnp.concatenate(q, 0))
        sg = 1.0 / (1.0 + jnp.exp(-v))
        dv = c_rd2 * (sg * (1.0 + v * (1.0 - sg)))
        dq = mixed(m2ts, m2th, dv) * 2.0
        for l in range(9):
            g = 0 if l == 0 else (1 if l < 4 else 2)
            m2[l, :, sl] = m2[l, :, sl] * dq[g * 128 : (g + 1) * 128]

    part[...] = jnp.zeros_like(part)

    @pl.loop(0, 16)
    def _(step):
        it = step // 4
        at = pl.multiple_of((step % 4) * 32, 32)
        rows_ = pl.ds(at, 32)
        rows_lo = pl.ds(at + 128, 32)
        lanes = pl.ds(pl.multiple_of(it * 128, 128), 128)
        dm = [m2[l, rows_, lanes] for l in range(9)]
        for k in range(8):
            g, w = gg[k, rows_, lanes], ww[k, rows_, lanes]
            car = g * w
            dcar = dm[0]
            for l in range(1, 9):
                dcar = dcar + y_row(l, k, it) * dm[l]
            for l in range(1, 9):
                pr = dm[l] * car
                pr = (pr[0:8] + pr[8:16]) + (pr[16:24] + pr[24:32])
                at8 = ((l - 1) * 8 + k) * 8
                part[at8 : at8 + 8, lanes] = part[at8 : at8 + 8, lanes] + pr
            edge = pl.ds(pl.multiple_of(k * 512 + it * 128, 128), 128)
            hi, lo = split(dcar * w)
            dg[rows_, edge] = hi
            dg[rows_lo, edge] = lo
            hi, lo = split(dcar * g)
            dw[rows_, edge] = hi
            dw[rows_lo, edge] = lo

    r2h, r2l = split(r2s)
    r2f = jnp.concatenate(
        [jnp.concatenate([r2h, r2h], 1).astype(F32), jnp.concatenate([r2l, jnp.zeros_like(r2l)], 1).astype(F32)], 0
    ).astype(BF16)
    for k in range(8):
        dbk = halves(dot(r2f, dw[:, k * 512 : (k + 1) * 512]))
        off, bk = basis(k)
        part[512 + k * 8 : 520 + k * 8, :] = -(dbk * bk * off)
    sel = (lax.broadcasted_iota(I32, (72, 576), 1) >> 3) == lax.broadcasted_iota(I32, (72, 576), 0)
    sel = jnp.where(sel, 1.0, 0.0).astype(BF16)
    ph, pl_ = split(part[...])
    two[...] = jnp.zeros_like(two)
    two[:, own_lanes] = dot(sel, ph) + dot(sel, pl_)

    @pl.loop(0, 4)
    def _(ch):
        at = pl.ds(pl.multiple_of(ch * 256, 256), 256)
        dh[:, at] = halves(dot_nt(dg[...], hot[at, :]))

    @pl.loop(0, 4)
    def _(ch):
        sl = pl.ds(pl.multiple_of(ch * 256, 256), 256)
        is_own = jnp.where(jnp.logical_or(ch == 1, ch == 2), 1.0, 0.0).astype(F32)
        dv = (dh[:, sl] + c_rd1 * is_own) * ds1[:, sl]
        dq = mixed(m1ts, m1th, dv) * 2.0
        on = geo[5, :, sl] > 0.5
        ux, uy, uz = geo[0, :, sl], geo[1, :, sl], geo[2, :, sl]
        s, inv = geo[3, :, sl], geo[4, :, sl]
        bs = [bb[n, :, sl] for n in range(8)]
        dy, db = [None], [None] * 8
        for l in range(9):
            g = 0 if l == 0 else (1 if l < 4 else 2)
            dm = m1[l, :, sl] * dq[g * 128 : (g + 1) * 128]
            dz = halves(dot(wtf, jnp.concatenate(split(dm), 0)))
            y = None if l == 0 else yy[l - 1, :, sl]
            acc = None
            for n in range(8):
                t = jnp.where(on, dz[64 + n * 8 : 72 + n * 8], dz[n * 8 : n * 8 + 8])
                if l == 0:
                    db[n] = t
                else:
                    db[n] = db[n] + t * y
                    acc = t * bs[n] if acc is None else acc + t * bs[n]
            if l:
                dy.append(acc + two[(l - 1) * 8 : l * 8, sl])
        dsv = two[64:72, sl]
        for n in range(8):
            dsv = dsv - db[n] * bs[n] * (s - (1.0 + n))
        dux = SQRT3 * dy[1] + SQRT15 * (uy * dy[4] + uz * dy[7] + ux * dy[8]) - SQRT5 * ux * dy[6]
        duy = SQRT3 * dy[2] + SQRT15 * (ux * dy[4] + uz * dy[5] - uy * dy[8]) - SQRT5 * uy * dy[6]
        duz = SQRT3 * dy[3] + SQRT15 * (uy * dy[5] + ux * dy[7]) + 2.0 * SQRT5 * uz * dy[6]
        along = dsv - (dux * ux + duy * uy + duz * uz) * inv
        dr[0, :, sl] = dux * inv + ux * along
        dr[1, :, sl] = duy * inv + uy * along
        dr[2, :, sl] = duz * inv + uz * along

    tile_ids = lax.broadcasted_iota(I32, (8, 1024), 0)
    lane_ids = lax.broadcasted_iota(I32, (128, 1024), 0)

    def onto(index_row, values):
        there = spread(index_row >> 7) == tile_ids
        his, los = [], []
        for v in values:
            m = jnp.where(there, spread(v), 0.0)
            hi = m.astype(BF16).astype(F32)
            his.append(hi)
            los.append(m - hi)
        lhs = jnp.concatenate(his + los, 0).astype(BF16)
        rhs = jnp.where(jnp.broadcast_to(index_row & 127, (128, 1024)) == lane_ids, 1.0, 0.0).astype(BF16)
        return lhs, rhs

    selfs = lax.broadcasted_iota(I32, (1, 1024), 1)
    lhs, rhs = onto(selfs, [-jnp.sum(dr[c], axis=0, keepdims=True) for c in range(3)])
    acc_own = dot_nt(lhs, rhs)
    acc_low = jnp.zeros((48, 128), F32)
    acc_up = jnp.zeros((48, 128), F32)
    for k in range(8):
        lhs, rhs = onto(nb_s[k : k + 1, :], [dr[c, k : k + 1, :] for c in range(3)])
        acc_own = acc_own + dot_nt(lhs[:, 256:768], rhs[:, 256:768])
        acc_low = acc_low + dot_nt(lhs[:, :256], rhs[:, :256])
        acc_up = acc_up + dot_nt(lhs[:, 768:], rhs[:, 768:])
    acc_own, acc_low, acc_up = halves(acc_own), halves(acc_low), halves(acc_up)

    def put(ref, at, acc, c, first, count):
        ref[at : at + count, :] = acc[c * 8 + first : c * 8 + first + count, :]

    for c in range(3):
        put(kept, c * 4, acc_own, c, 2, 4)
        put(kept, 12 + c * 4, acc_low, c, 6, 2)
        put(kept, 14 + c * 4, acc_up, c, 0, 2)
        put(to_low, c * 4, acc_low, c, 2, 4)
        put(to_low, 12 + c * 2, acc_own, c, 0, 2)
        put(to_up, c * 4, acc_up, c, 2, 4)
        put(to_up, 12 + c * 2, acc_own, c, 6, 2)
        put(to_low2, c * 2, acc_low, c, 0, 2)
        put(to_up2, c * 2, acc_up, c, 6, 2)
    pad2, pad6 = jnp.zeros((2, 128), F32), jnp.zeros((6, 128), F32)
    to_low[18:24, :] = pad6
    to_up[18:24, :] = pad6
    to_low2[6:8, :] = pad2
    to_up2[6:8, :] = pad2


COMPUTE_SCRATCH = [
    pltpu.VMEM((8, 1024), I32),
    pltpu.VMEM((6, 8, 1024), F32),
    pltpu.VMEM((8, 8, 1024), F32),
    pltpu.VMEM((8, 8, 1024), F32),
    pltpu.VMEM((1024, 4096), BF16),
    pltpu.VMEM((9, 128, 1024), F32),
    pltpu.VMEM((256, 1024), BF16),
    pltpu.VMEM((128, 1024), F32),
    pltpu.VMEM((8, 128, 512), F32),
    pltpu.VMEM((8, 128, 512), F32),
    pltpu.VMEM((9, 128, 512), F32),
    pltpu.VMEM((256, 4096), BF16),
    pltpu.VMEM((256, 4096), BF16),
    pltpu.VMEM((576, 512), F32),
    pltpu.VMEM((72, 1024), F32),
    pltpu.VMEM((128, 1024), F32),
    pltpu.VMEM((3, 8, 1024), F32),
    pltpu.VMEM((8, 1024), F32),
]


def compute(own, low1, up1, low2, up2, emb, r1, r2, mix1, mix2, rd1, rd2):
    shape = lambda n: jax.ShapeDtypeStruct((n, 128), F32)
    return pl.pallas_call(
        compute_kernel,
        out_shape=(shape(24), shape(24), shape(8), shape(8), shape(24)),
        in_specs=[VM] * 12,
        out_specs=(VM,) * 5,
        scratch_shapes=COMPUTE_SCRATCH,
        compiler_params=pltpu.CompilerParams(vmem_limit_bytes=60 << 20),
        name="energy_gradient",
    )(own, low1, up1, low2, up2, emb, r1, r2, mix1, mix2, rd1, rd2)


def halo_kernel(domains, mine, low1, up1, low2, up2, send_sem, recv_sem):
    me = lax.axis_index("space")
    peers = [lax.rem(me + s + domains, domains) for s in (1, -1, 2, -2)]
    barrier = pltpu.get_barrier_semaphore()
    for p in peers:
        pl.semaphore_signal(barrier, inc=1, device_id={"space": p}, device_id_type=MESH)
    pl.semaphore_wait(barrier, 4)
    src = (mine, mine, mine.at[0:8], mine.at[0:8])
    copies = []
    for i, (p, s, dst) in enumerate(zip(peers, src, (low1, up1, low2, up2))):
        copies.append(
            pltpu.make_async_remote_copy(
                src_ref=s, dst_ref=dst, send_sem=send_sem.at[i], recv_sem=recv_sem.at[i],
                device_id={"space": p}, device_id_type=MESH,
            )
        )
        copies[-1].start()
    for c in copies:
        c.wait()


def halo(mine, domains):
    shape = lambda n: jax.ShapeDtypeStruct((n, 512), F32)
    return pl.pallas_call(
        lambda *refs: halo_kernel(domains, *refs),
        out_shape=(shape(16), shape(16), shape(8), shape(8)),
        in_specs=[VM],
        out_specs=(VM,) * 4,
        scratch_shapes=[pltpu.SemaphoreType.DMA((4,)), pltpu.SemaphoreType.DMA((4,))],
        compiler_params=pltpu.CompilerParams(collective_id=0, has_side_effects=True),
        name="halo",
    )(mine)


def ring_tables(beads):
    b = np.arange(beads, dtype=np.float64)
    angle = beads * np.sin(np.pi * b / beads)
    safe = np.where(b == 0, 1.0, angle)
    reach = np.where(b == 0, STEP, STEP * np.sin(angle) / safe)
    stiff = angle * np.sin(angle) / STEP
    phase = np.cos(2.0 * np.pi * np.outer(b, b) / beads) / beads
    return [(phase @ f).tolist() for f in (np.cos(angle), reach, stiff)]


def rows12(ref):
    return jnp.concatenate([ref[c : c + 1, t * 128 : (t + 1) * 128] for c in range(3) for t in range(4)], 0)


def finish_kernel(
    domains, beads,
    to_low, to_up, to_low2, to_up2, kept, pos, mom, mine,
    new_pos, new_mom,
    from_low, from_up, from_low2, from_up2, q_src, p_src, q_all, p_all,
    hs_sem, hr_sem, qs_sem, qr_sem, ps_sem, pr_sem,
):
    me = lax.axis_index("space")
    bead = lax.axis_index("bead")
    near = [lax.rem(me + s + domains, domains) for s in (1, -1, 2, -2)]
    ring = [lax.rem(bead + o, beads) for o in range(beads)]
    barrier = pltpu.get_barrier_semaphore()
    for p in near:
        pl.semaphore_signal(barrier, inc=1, device_id={"space": p}, device_id_type=MESH)
    for o in range(1, beads):
        pl.semaphore_signal(barrier, inc=1, device_id={"bead": ring[o]}, device_id_type=MESH)
    q_src[...] = rows12(pos)
    pl.semaphore_wait(barrier, 4 + beads - 1)

    copies = []
    for i, (p, s, dst) in enumerate(
        zip(near, (to_up, to_low, to_up2, to_low2), (from_low, from_up, from_low2, from_up2))
    ):
        copies.append(
            pltpu.make_async_remote_copy(
                src_ref=s, dst_ref=dst, send_sem=hs_sem.at[i], recv_sem=hr_sem.at[i],
                device_id={"space": p}, device_id_type=MESH,
            )
        )
        copies[-1].start()

    def share(src, dst, s_sem, r_sem):
        out = []
        for o in range(1, beads):
            c = pltpu.make_async_remote_copy(
                src_ref=src, dst_ref=dst.at[o], send_sem=s_sem.at[o], recv_sem=r_sem.at[o],
                device_id={"bead": ring[o]}, device_id_type=MESH,
            )
            c.start()
            out.append(c)
        return out

    q_copies = share(q_src, q_all, qs_sem, qr_sem)
    send = mine[4:5, :].astype(I32)
    there = [spread(send[:, t * 128 : (t + 1) * 128] >> 7) for t in range(4)]
    iota8 = lax.broadcasted_iota(I32, (8, 128), 0)
    rhs = jnp.where(
        jnp.broadcast_to(send & 127, (128, 512)) == lax.broadcasted_iota(I32, (128, 512), 0), 1.0, 0.0
    ).astype(BF16)
    mass4 = HEAVY - (HEAVY - 1.0) * jnp.concatenate(
        [mine[3:4, t * 128 : (t + 1) * 128] for t in range(4)], 0
    )
    mass = jnp.concatenate([mass4, mass4, mass4], 0)
    p12 = rows12(mom)
    for c in copies:
        c.wait()

    his, los = [], []
    for c in range(3):
        parts = []
        for t in range(4):
            near_, far = (from_low, from_low2) if t < 2 else (from_up, from_up2)
            at, a12, a2 = 12 + c * 4 + t, 12 + c * 2 + t % 2, c * 2 + t % 2
            v = kept[at : at + 1, :] + near_[a12 : a12 + 1, :] + far[a2 : a2 + 1, :]
            parts.append(jnp.where(there[t] == iota8, spread(v), 0.0))
        m = jnp.concatenate(parts, 1)
        hi = m.astype(BF16).astype(F32)
        his.append(hi)
        los.append(m - hi)
    got = halves(dot_nt(jnp.concatenate(his + los, 0).astype(BF16), rhs))
    got = jnp.concatenate([got[c * 8 : c * 8 + 4] for c in range(3)], 0)
    kicked = p12 - (kept[0:12, :] + from_low[0:12, :] + from_up[0:12, :] + got)
    p_src[...] = kicked
    p_copies = share(p_src, p_all, ps_sem, pr_sem)

    turn, reach, stiff = ring_tables(beads)
    q = q_src[...]
    qa, qs = turn[0] * q, stiff[0] * q
    for o, c in zip(range(1, beads), q_copies):
        c.wait()
        q = q_all[o]
        qa, qs = qa + turn[o] * q, qs + stiff[o] * q
    pa, pr = turn[0] * kicked, reach[0] * kicked
    for o, c in zip(range(1, beads), p_copies):
        c.wait()
        p = p_all[o]
        pa, pr = pa + turn[o] * p, pr + reach[o] * p
    qn = qa + pr / mass
    pn = pa - mass * qs
    for c in range(3):
        for t in range(4):
            at = c * 4 + t
            new_pos[c : c + 1, t * 128 : (t + 1) * 128] = qn[at : at + 1]
            new_mom[c : c + 1, t * 128 : (t + 1) * 128] = pn[at : at + 1]


def finish(pieces, pos, mom, mine, domains, beads):
    dma = lambda n: pltpu.SemaphoreType.DMA((n,))
    return pl.pallas_call(
        lambda *refs: finish_kernel(domains, beads, *refs),
        out_shape=(jax.ShapeDtypeStruct((3, 512), F32),) * 2,
        in_specs=[VM] * 8,
        out_specs=(VM,) * 2,
        scratch_shapes=[
            pltpu.VMEM((24, 128), F32), pltpu.VMEM((24, 128), F32),
            pltpu.VMEM((8, 128), F32), pltpu.VMEM((8, 128), F32),
            pltpu.VMEM((12, 128), F32), pltpu.VMEM((12, 128), F32),
            pltpu.VMEM((beads, 12, 128), F32), pltpu.VMEM((beads, 12, 128), F32),
            dma(4), dma(4), dma(beads), dma(beads), dma(beads), dma(beads),
        ],
        compiler_params=pltpu.CompilerParams(collective_id=1, has_side_effects=True),
        name="finish",
    )(*pieces, pos, mom, mine)


def shards(
    positions, momenta, species, neighbours, send_list, embedding,
    radial_one, radial_two, mix_one, mix_two, read_one, read_two,
):
    domains, beads = lax.axis_size("space"), lax.axis_size("bead")
    mine = jnp.concatenate(
        [
            positions[0], species.astype(F32)[None], send_list.astype(F32)[None],
            jnp.zeros((3, 512), F32), neighbours.astype(F32),
        ],
        0,
    )
    near = halo(mine, domains)
    pieces = compute(
        mine, *near, embedding, radial_one, radial_two, mix_one, mix_two, read_one[None], read_two[None]
    )
    q, p = finish(pieces, positions[0], momenta[0], mine, domains, beads)
    return q[None], p[None]


def solution(mesh):
    beads = P("bead", None, "space")
    placed = (beads, beads, P("space"), P(None, "space"), P("space")) + (P(),) * 7
    return jax.shard_map(shards, mesh=mesh, in_specs=placed, out_specs=(beads, beads), check_vma=False)
```

```python
import math

import numpy as np

import jax
import jax.numpy as jnp
from jax import lax
from jax.experimental import pallas as pl
from jax.experimental.pallas import tpu as pltpu
from jax.sharding import PartitionSpec as P

STEP = 2.0
HEAVY = 16.0
SQRT3 = math.sqrt(3.0)
SQRT5 = math.sqrt(5.0)
SQRT15 = math.sqrt(15.0)
F32 = jnp.float32
BF16 = jnp.bfloat16
I32 = jnp.int32
NT = (((1,), (1,)), ((), ()))
VM = pl.BlockSpec(memory_space=pltpu.VMEM)
SM = pl.BlockSpec(memory_space=pltpu.SMEM)
MESH = pl.DeviceIdType.MESH


def dot(a, b):
    return jnp.dot(a, b, preferred_element_type=F32)


def dot_nt(a, b):
    return lax.dot_general(a, b, NT, preferred_element_type=F32)


def split(x):
    hi = x.astype(BF16)
    return hi, (x - hi.astype(F32)).astype(BF16)


def halves(x):
    n = x.shape[0] // 2
    return x[:n] + x[n:]


def lane_take(tiles, idx):
    low = idx & 127
    high = idx >> 7
    out = jnp.take_along_axis(tiles[0], low, axis=1)
    for t in range(1, len(tiles)):
        out = jnp.where(high == t, jnp.take_along_axis(tiles[t], low, axis=1), out)
    return out


def spread(row, count=8):
    return jnp.broadcast_to(row, (count, row.shape[1]))


def build_hot(nbr, hot):
    @pl.loop(0, 8)
    def _(rc):
        at = pl.multiple_of(rc * 128, 128)
        ids = lax.broadcasted_iota(I32, (128, 512), 0) + at
        for k in range(8):
            row = jnp.broadcast_to(nbr[k : k + 1, :], (128, 512))
            hot[pl.ds(at, 128), k * 512 : (k + 1) * 512] = jnp.where(ids == row, 1.0, 0.0).astype(BF16)


def energy_gradient(
    ext_own, ext_low, ext_up, nb_t, emb, r1, r2, mix1, mix2, rd1, rd2,
    to_low, to_up, to_low2, to_up2, kept,
    nb_s, geo, yy, bb, hot, m1, hs, ds1, gg, ww, m2, dg, dw, part, two, dh, dr, fl,
):
    for e in range(8):
        cols = slice(e * 128, (e + 1) * 128)
        ext = ext_low if e < 2 else (ext_own if e < 6 else ext_up)
        idx = nb_t[e]
        nb_s[:, cols] = idx
        fl[:, cols] = spread(ext_own[e][3:4])
        got = [lane_take([spread(x[c : c + 1]) for x in ext], idx) for c in range(4)]
        rx, ry, rz = [got[c] - spread(ext_own[e][c : c + 1]) for c in range(3)]
        s = jnp.sqrt(rx * rx + ry * ry + rz * rz + 1.0)
        inv = 1.0 / s
        ux, uy, uz = rx * inv, ry * inv, rz * inv
        for c, v in enumerate((ux, uy, uz, s, inv, got[3])):
            geo[c, :, cols] = v
        ys = (
            SQRT3 * ux, SQRT3 * uy, SQRT3 * uz,
            SQRT15 * ux * uy, SQRT15 * uy * uz,
            0.5 * SQRT5 * (2.0 * uz * uz - ux * ux - uy * uy),
            SQRT15 * ux * uz, 0.5 * SQRT15 * (ux * ux - uy * uy),
        )
        for l in range(8):
            yy[l, :, cols] = ys[l]
        for n in range(8):
            bb[n, :, cols] = jnp.exp(-0.5 * (s - (1.0 + n)) ** 2)

    w_rows = []
    for f in range(2):
        for n in range(8):
            w_rows.append(spread(r1[n : n + 1, :] * emb[f : f + 1, :] * 0.125))
    wt = jnp.concatenate(w_rows, axis=0)
    wth, wtl = split(wt)
    wh, wl = split(jnp.transpose(wt))
    zero = jnp.zeros((128, 128), BF16)
    wf = jnp.concatenate([jnp.concatenate([wh, wh], 1), jnp.concatenate([wl, zero], 1)], 0)
    wtf = jnp.concatenate([jnp.concatenate([wth, wth], 1), jnp.concatenate([wtl, zero], 1)], 0)
    r2s = r2[...] * 0.125
    rows = jnp.concatenate([emb[...], rd1[...], rd2[...], jnp.zeros((4, 128), F32), r2s], 0)
    colmat = jnp.transpose(jnp.concatenate([rows, jnp.zeros((112, 128), F32)], 0))
    e0, e1 = colmat[:, 0:1], colmat[:, 1:2]
    c_rd1, c_rd2 = colmat[:, 2:3], colmat[:, 3:4]
    m1h, m1l = split(mix1[...])
    m1s = jnp.concatenate([m1h, m1l], 0)
    m1t = jnp.transpose(mix1[...])
    m1th, m1tl = split(m1t)
    m1ts = jnp.concatenate([m1th, m1tl], 0)
    m2h, m2l = split(mix2[...])
    m2s = jnp.concatenate([m2h, m2l], 0)
    m2th, m2tl = split(jnp.transpose(mix2[...]))
    m2ts = jnp.concatenate([m2th, m2tl], 0)

    def mixed(ws, wh_, x):
        hi, lo = split(x)
        return halves(dot(ws, hi)) + dot(wh_, lo)

    @pl.loop(0, 4)
    def _(ch):
        sl = pl.ds(pl.multiple_of(ch * 256, 256), 256)
        f = geo[5, :, sl]
        bs = []
        for n in range(8):
            bs.append(bb[n, :, sl] * (1.0 - f))
        for n in range(8):
            bs.append(bb[n, :, sl] * f)
        q = [None, None, None]
        for l in range(9):
            z = jnp.concatenate(bs if l == 0 else [yy[l - 1, :, sl] * b for b in bs], 0)
            m = halves(dot(wf, jnp.concatenate(split(z), 0)))
            m1[l, :, sl] = m
            g = 0 if l == 0 else (1 if l < 4 else 2)
            q[g] = m * m if q[g] is None else q[g] + m * m
        v = mixed(m1s, m1h, jnp.concatenate(q, 0))
        sg = 1.0 / (1.0 + jnp.exp(-v))
        fc = fl[0:1, sl]
        h = e0 + fc * (e1 - e0) + v * sg
        ds1[:, sl] = sg * (1.0 + v * (1.0 - sg))
        hs[:, sl] = jnp.concatenate(split(h), 0)

    own_lanes = slice(256, 768)
    iota8 = lax.broadcasted_iota(I32, (8, 512), 0).astype(F32)
    r2th, r2tl = split(colmat[:, 8:16])
    r2lhs = jnp.concatenate([r2th.astype(F32), r2th.astype(F32), r2tl.astype(F32)], 1).astype(BF16)

    def basis(k):
        off = spread(geo[3, k : k + 1, own_lanes]) - 1.0 - iota8
        return off, jnp.exp(-0.5 * off * off)

    for k in range(8):
        gg[k] = halves(dot(hs[...], hot[:, k * 512 : (k + 1) * 512]))
        _, bk = basis(k)
        bh, bl = split(bk)
        rhs = jnp.concatenate([bh.astype(F32), bl.astype(F32), bh.astype(F32)], 0).astype(BF16)
        ww[k] = dot(r2lhs, rhs)

    def y_row(l, k, it):
        at = pl.multiple_of(256 + it * 128, 128)
        return yy[l - 1, k : k + 1, pl.ds(at, 128)]

    @pl.loop(0, 16)
    def _(step):
        it = step // 4
        rows_ = pl.ds(pl.multiple_of((step % 4) * 32, 32), 32)
        lanes = pl.ds(pl.multiple_of(it * 128, 128), 128)
        car = [gg[k, rows_, lanes] * ww[k, rows_, lanes] for k in range(8)]
        acc = car[0]
        for k in range(1, 8):
            acc = acc + car[k]
        m2[0, rows_, lanes] = acc
        for l in range(1, 9):
            acc = y_row(l, 0, it) * car[0]
            for k in range(1, 8):
                acc = acc + y_row(l, k, it) * car[k]
            m2[l, rows_, lanes] = acc

    @pl.loop(0, 2)
    def _(ch):
        sl = pl.ds(pl.multiple_of(ch * 256, 256), 256)
        q = [None, None, None]
        for l in range(9):
            m = m2[l, :, sl]
            g = 0 if l == 0 else (1 if l < 4 else 2)
            q[g] = m * m if q[g] is None else q[g] + m * m
        v = mixed(m2s, m2h, jnp.concatenate(q, 0))
        sg = 1.0 / (1.0 + jnp.exp(-v))
        dv = c_rd2 * (sg * (1.0 + v * (1.0 - sg)))
        dq = mixed(m2ts, m2th, dv) * 2.0
        for l in range(9):
            g = 0 if l == 0 else (1 if l < 4 else 2)
            m2[l, :, sl] = m2[l, :, sl] * dq[g * 128 : (g + 1) * 128]

    part[...] = jnp.zeros_like(part)

    @pl.loop(0, 16)
    def _(step):
        it = step // 4
        at = pl.multiple_of((step % 4) * 32, 32)
        rows_ = pl.ds(at, 32)
        rows_lo = pl.ds(at + 128, 32)
        lanes = pl.ds(pl.multiple_of(it * 128, 128), 128)
        dm = [m2[l, rows_, lanes] for l in range(9)]
        for k in range(8):
            g, w = gg[k, rows_, lanes], ww[k, rows_, lanes]
            car = g * w
            dcar = dm[0]
            for l in range(1, 9):
                dcar = dcar + y_row(l, k, it) * dm[l]
            for l in range(1, 9):
                pr = dm[l] * car
                pr = (pr[0:8] + pr[8:16]) + (pr[16:24] + pr[24:32])
                at8 = ((l - 1) * 8 + k) * 8
                part[at8 : at8 + 8, lanes] = part[at8 : at8 + 8, lanes] + pr
            edge = pl.ds(pl.multiple_of(k * 512 + it * 128, 128), 128)
            hi, lo = split(dcar * w)
            dg[rows_, edge] = hi
            dg[rows_lo, edge] = lo
            hi, lo = split(dcar * g)
            dw[rows_, edge] = hi
            dw[rows_lo, edge] = lo

    r2h, r2l = split(r2s)
    r2f = jnp.concatenate(
        [jnp.concatenate([r2h, r2h], 1).astype(F32), jnp.concatenate([r2l, jnp.zeros_like(r2l)], 1).astype(F32)], 0
    ).astype(BF16)
    for k in range(8):
        dbk = halves(dot(r2f, dw[:, k * 512 : (k + 1) * 512]))
        off, bk = basis(k)
        part[512 + k * 8 : 520 + k * 8, :] = -(dbk * bk * off)
    sel = (lax.broadcasted_iota(I32, (72, 576), 1) >> 3) == lax.broadcasted_iota(I32, (72, 576), 0)
    sel = jnp.where(sel, 1.0, 0.0).astype(BF16)
    ph, pl_ = split(part[...])
    two[...] = jnp.zeros_like(two)
    two[:, own_lanes] = dot(sel, ph) + dot(sel, pl_)

    @pl.loop(0, 4)
    def _(ch):
        at = pl.ds(pl.multiple_of(ch * 256, 256), 256)
        dh[:, at] = halves(dot_nt(dg[...], hot[at, :]))

    @pl.loop(0, 4)
    def _(ch):
        sl = pl.ds(pl.multiple_of(ch * 256, 256), 256)
        is_own = jnp.where(jnp.logical_or(ch == 1, ch == 2), 1.0, 0.0).astype(F32)
        dv = (dh[:, sl] + c_rd1 * is_own) * ds1[:, sl]
        dq = mixed(m1ts, m1th, dv) * 2.0
        on = geo[5, :, sl] > 0.5
        ux, uy, uz = geo[0, :, sl], geo[1, :, sl], geo[2, :, sl]
        s, inv = geo[3, :, sl], geo[4, :, sl]
        bs = [bb[n, :, sl] for n in range(8)]
        dy, db = [None], [None] * 8
        for l in range(9):
            g = 0 if l == 0 else (1 if l < 4 else 2)
            dm = m1[l, :, sl] * dq[g * 128 : (g + 1) * 128]
            dz = halves(dot(wtf, jnp.concatenate(split(dm), 0)))
            y = None if l == 0 else yy[l - 1, :, sl]
            acc = None
            for n in range(8):
                t = jnp.where(on, dz[64 + n * 8 : 72 + n * 8], dz[n * 8 : n * 8 + 8])
                if l == 0:
                    db[n] = t
                else:
                    db[n] = db[n] + t * y
                    acc = t * bs[n] if acc is None else acc + t * bs[n]
            if l:
                dy.append(acc + two[(l - 1) * 8 : l * 8, sl])
        dsv = two[64:72, sl]
        for n in range(8):
            dsv = dsv - db[n] * bs[n] * (s - (1.0 + n))
        dux = SQRT3 * dy[1] + SQRT15 * (uy * dy[4] + uz * dy[7] + ux * dy[8]) - SQRT5 * ux * dy[6]
        duy = SQRT3 * dy[2] + SQRT15 * (ux * dy[4] + uz * dy[5] - uy * dy[8]) - SQRT5 * uy * dy[6]
        duz = SQRT3 * dy[3] + SQRT15 * (uy * dy[5] + ux * dy[7]) + 2.0 * SQRT5 * uz * dy[6]
        along = dsv - (dux * ux + duy * uy + duz * uz) * inv
        dr[0, :, sl] = dux * inv + ux * along
        dr[1, :, sl] = duy * inv + uy * along
        dr[2, :, sl] = duz * inv + uz * along

    tile_ids = lax.broadcasted_iota(I32, (8, 1024), 0)
    lane_ids = lax.broadcasted_iota(I32, (128, 1024), 0)

    def onto(index_row, values):
        there = spread(index_row >> 7) == tile_ids
        his, los = [], []
        for v in values:
            m = jnp.where(there, spread(v), 0.0)
            hi = m.astype(BF16).astype(F32)
            his.append(hi)
            los.append(m - hi)
        lhs = jnp.concatenate(his + los, 0).astype(BF16)
        rhs = jnp.where(jnp.broadcast_to(index_row & 127, (128, 1024)) == lane_ids, 1.0, 0.0).astype(BF16)
        return lhs, rhs

    selfs = lax.broadcasted_iota(I32, (1, 1024), 1)
    lhs, rhs = onto(selfs, [-jnp.sum(dr[c], axis=0, keepdims=True) for c in range(3)])
    acc_own = dot_nt(lhs, rhs)
    acc_low = jnp.zeros((48, 128), F32)
    acc_up = jnp.zeros((48, 128), F32)
    for k in range(8):
        lhs, rhs = onto(nb_s[k : k + 1, :], [dr[c, k : k + 1, :] for c in range(3)])
        acc_own = acc_own + dot_nt(lhs[:, 256:768], rhs[:, 256:768])
        acc_low = acc_low + dot_nt(lhs[:, :256], rhs[:, :256])
        acc_up = acc_up + dot_nt(lhs[:, 768:], rhs[:, 768:])
    acc_own, acc_low, acc_up = halves(acc_own), halves(acc_low), halves(acc_up)

    def put(ref, at, acc, c, first, count):
        ref[at : at + count, :] = acc[c * 8 + first : c * 8 + first + count, :]

    for c in range(3):
        put(kept, c * 4, acc_own, c, 2, 4)
        put(kept, 12 + c * 4, acc_low, c, 6, 2)
        put(kept, 14 + c * 4, acc_up, c, 0, 2)
        put(to_low, c * 4, acc_low, c, 2, 4)
        put(to_low, 12 + c * 2, acc_own, c, 0, 2)
        put(to_up, c * 4, acc_up, c, 2, 4)
        put(to_up, 12 + c * 2, acc_own, c, 6, 2)
        put(to_low2, c * 2, acc_low, c, 0, 2)
        put(to_up2, c * 2, acc_up, c, 6, 2)
    pad2, pad6 = jnp.zeros((2, 128), F32), jnp.zeros((6, 128), F32)
    to_low[18:24, :] = pad6
    to_up[18:24, :] = pad6
    to_low2[6:8, :] = pad2
    to_up2[6:8, :] = pad2


COMPUTE_SCRATCH = [
    pltpu.VMEM((8, 1024), I32),
    pltpu.VMEM((6, 8, 1024), F32),
    pltpu.VMEM((8, 8, 1024), F32),
    pltpu.VMEM((8, 8, 1024), F32),
    pltpu.VMEM((1024, 4096), BF16),
    pltpu.VMEM((9, 128, 1024), F32),
    pltpu.VMEM((256, 1024), BF16),
    pltpu.VMEM((128, 1024), F32),
    pltpu.VMEM((8, 128, 512), F32),
    pltpu.VMEM((8, 128, 512), F32),
    pltpu.VMEM((9, 128, 512), F32),
    pltpu.VMEM((256, 4096), BF16),
    pltpu.VMEM((256, 4096), BF16),
    pltpu.VMEM((576, 512), F32),
    pltpu.VMEM((72, 1024), F32),
    pltpu.VMEM((128, 1024), F32),
    pltpu.VMEM((3, 8, 1024), F32),
    pltpu.VMEM((8, 1024), F32),
]


def ring_tables(beads):
    b = np.arange(beads, dtype=np.float64)
    angle = beads * np.sin(np.pi * b / beads)
    safe = np.where(b == 0, 1.0, angle)
    reach = np.where(b == 0, STEP, STEP * np.sin(angle) / safe)
    stiff = angle * np.sin(angle) / STEP
    phase = np.cos(2.0 * np.pi * np.outer(b, b) / beads) / beads
    return [(phase @ f).tolist() for f in (np.cos(angle), reach, stiff)]


def rows12(ref):
    return jnp.concatenate([ref[c, 0:1, t * 128 : (t + 1) * 128] for c in range(3) for t in range(4)], 0)


def step_kernel(
    domains, beads,
    pos, mom, spec, nbr, send_ref, emb, r1, r2, mix1, mix2, rd1, rd2,
    new_pos, new_mom,
    msg_up, msg_low, in_low, in_up, in_low2, in_up2,
    to_low, to_up, to_low2, to_up2, kept,
    from_low, from_up, from_low2, from_up2, q_src, p_src, q_all, p_all,
    fs_sem, fr_sem, hs_sem, hr_sem, qs_sem, qr_sem, ps_sem, pr_sem,
    *work,
):
    me = lax.axis_index("space")
    bead = lax.axis_index("bead")
    near = [lax.rem(me + s + domains, domains) for s in (1, -1, 2, -2)]
    ring = [lax.rem(bead + o, beads) for o in range(beads)]
    barrier = pltpu.get_barrier_semaphore()
    for p in near:
        pl.semaphore_signal(barrier, inc=1, device_id={"space": p}, device_id_type=MESH)
    for o in range(1, beads):
        pl.semaphore_signal(barrier, inc=1, device_id={"bead": ring[o]}, device_id_type=MESH)

    flags = spec[...].astype(F32)
    send = send_ref[...]
    own_t, nbr_t = [], []
    for t in range(4):
        lanes = slice(t * 128, (t + 1) * 128)
        quad = [pos[c, 0:1, lanes] for c in range(3)] + [flags[:, lanes]]
        own_t.append(jnp.concatenate(quad + quad, 0))
        nbr_t.append(nbr[:, lanes])

    def sent(tiles, half):
        return [
            lane_take(tiles, spread(send[:, at : at + 128])) for at in (half * 256, half * 256 + 128)
        ]

    def pair(x, y):
        return jnp.concatenate([x[0:4], y[4:8]], 0)

    def both(x):
        return [jnp.concatenate([x[0:4], x[0:4]], 0), jnp.concatenate([x[4:8], x[4:8]], 0)]

    ghosts = [sent(own_t, 0), sent(own_t, 1)]
    q_src[...] = rows12(pos)
    for msg, half in ((msg_low, 0), (msg_up, 1)):
        lists = sent(nbr_t, half)
        msg[0:8, :] = pair(own_t[0], own_t[1])
        msg[8:16, :] = pair(own_t[2], own_t[3])
        msg[16:24, :] = pair(*ghosts[half])
        msg[24:32, :] = lists[0].astype(F32)
        msg[32:40, :] = lists[1].astype(F32)
    pl.semaphore_wait(barrier, 4 + beads - 1)

    def to_near(srcs, dsts, s_sem, r_sem):
        out = []
        for i, (p, s, dst) in enumerate(zip(near, srcs, dsts)):
            c = pltpu.make_async_remote_copy(
                src_ref=s, dst_ref=dst, send_sem=s_sem.at[i], recv_sem=r_sem.at[i],
                device_id={"space": p}, device_id_type=MESH,
            )
            c.start()
            out.append(c)
        return out

    def share(src, dst, s_sem, r_sem):
        out = []
        for o in range(1, beads):
            c = pltpu.make_async_remote_copy(
                src_ref=src, dst_ref=dst.at[o], send_sem=s_sem.at[o], recv_sem=r_sem.at[o],
                device_id={"bead": ring[o]}, device_id_type=MESH,
            )
            c.start()
            out.append(c)
        return out

    halo = to_near(
        (msg_up, msg_low, msg_up.at[16:24], msg_low.at[16:24]), (in_low, in_up, in_low2, in_up2), fs_sem, fr_sem
    )
    build_hot(nbr, work[4])
    for c in halo:
        c.wait()
    q_copies = share(q_src, q_all, qs_sem, qr_sem)

    def whole(ref):
        return both(ref[0:8, :]) + both(ref[8:16, :])

    ext_own = both(in_low[16:24, :]) + own_t + both(in_up[16:24, :])
    ext_low = both(in_low2[...]) + whole(in_low) + ghosts[0]
    ext_up = ghosts[1] + whole(in_up) + both(in_up2[...])
    nb_t = [in_low[24:32, :].astype(I32), in_low[32:40, :].astype(I32)] + nbr_t
    nb_t = nb_t + [in_up[24:32, :].astype(I32), in_up[32:40, :].astype(I32)]
    energy_gradient(
        ext_own, ext_low, ext_up, nb_t, emb, r1, r2, mix1, mix2, rd1, rd2,
        to_low, to_up, to_low2, to_up2, kept, *work,
    )
    copies = to_near(
        (to_up, to_low, to_up2, to_low2), (from_low, from_up, from_low2, from_up2), hs_sem, hr_sem
    )

    there = [spread(send[:, t * 128 : (t + 1) * 128] >> 7) for t in range(4)]
    iota8 = lax.broadcasted_iota(I32, (8, 128), 0)
    rhs = jnp.where(
        jnp.broadcast_to(send & 127, (128, 512)) == lax.broadcasted_iota(I32, (128, 512), 0), 1.0, 0.0
    ).astype(BF16)
    mass4 = HEAVY - (HEAVY - 1.0) * jnp.concatenate(
        [flags[:, t * 128 : (t + 1) * 128] for t in range(4)], 0
    )
    mass = jnp.concatenate([mass4, mass4, mass4], 0)
    p12 = rows12(mom)
    for c in copies:
        c.wait()

    his, los = [], []
    for c in range(3):
        parts = []
        for t in range(4):
            near_, far = (from_low, from_low2) if t < 2 else (from_up, from_up2)
            at, a12, a2 = 12 + c * 4 + t, 12 + c * 2 + t % 2, c * 2 + t % 2
            v = kept[at : at + 1, :] + near_[a12 : a12 + 1, :] + far[a2 : a2 + 1, :]
            parts.append(jnp.where(there[t] == iota8, spread(v), 0.0))
        m = jnp.concatenate(parts, 1)
        hi = m.astype(BF16).astype(F32)
        his.append(hi)
        los.append(m - hi)
    got = halves(dot_nt(jnp.concatenate(his + los, 0).astype(BF16), rhs))
    got = jnp.concatenate([got[c * 8 : c * 8 + 4] for c in range(3)], 0)
    kicked = p12 - (kept[0:12, :] + from_low[0:12, :] + from_up[0:12, :] + got)
    p_src[...] = kicked
    p_copies = share(p_src, p_all, ps_sem, pr_sem)

    turn, reach, stiff = ring_tables(beads)
    q = q_src[...]
    qa, qs = turn[0] * q, stiff[0] * q
    for o, c in zip(range(1, beads), q_copies):
        c.wait()
        q = q_all[o]
        qa, qs = qa + turn[o] * q, qs + stiff[o] * q
    pa, pr = turn[0] * kicked, reach[0] * kicked
    for o, c in zip(range(1, beads), p_copies):
        c.wait()
        p = p_all[o]
        pa, pr = pa + turn[o] * p, pr + reach[o] * p
    qn = qa + pr / mass
    pn = pa - mass * qs
    for c in range(3):
        for t in range(4):
            at = c * 4 + t
            new_pos[c, 0:1, t * 128 : (t + 1) * 128] = qn[at : at + 1]
            new_mom[c, 0:1, t * 128 : (t + 1) * 128] = pn[at : at + 1]


def shards(
    positions, momenta, species, neighbours, send_list, embedding,
    radial_one, radial_two, mix_one, mix_two, read_one, read_two,
):
    domains, beads = lax.axis_size("space"), lax.axis_size("bead")
    dma = lambda n: pltpu.SemaphoreType.DMA((n,))
    rows = lambda n: pltpu.VMEM((n, 128), F32)
    q, p = pl.pallas_call(
        lambda *refs: step_kernel(domains, beads, *refs),
        out_shape=(jax.ShapeDtypeStruct((3, 1, 512), F32),) * 2,
        in_specs=[VM] * 12,
        out_specs=(VM,) * 2,
        scratch_shapes=[rows(n) for n in (40, 40, 40, 40, 8, 8, 24, 24, 8, 8, 24, 24, 24, 8, 8, 12, 12)]
        + [pltpu.VMEM((beads, 12, 128), F32)] * 2
        + [dma(4)] * 4 + [dma(beads)] * 4 + COMPUTE_SCRATCH,
        compiler_params=pltpu.CompilerParams(
            collective_id=0, has_side_effects=True, vmem_limit_bytes=60 << 20
        ),
        name="md_step",
    )(
        jnp.transpose(positions, (1, 0, 2)), jnp.transpose(momenta, (1, 0, 2)), species[None], neighbours,
        send_list[None], embedding, radial_one, radial_two, mix_one, mix_two, read_one[None], read_two[None],
    )
    return jnp.transpose(q, (1, 0, 2)), jnp.transpose(p, (1, 0, 2))


def solution(mesh):
    beads = P("bead", None, "space")
    placed = (beads, beads, P("space"), P(None, "space"), P("space")) + (P(),) * 7
    return jax.shard_map(shards, mesh=mesh, in_specs=placed, out_specs=(beads, beads), check_vma=False)
```

```python
import math

import numpy as np

import jax
import jax.numpy as jnp
from jax import lax
from jax.experimental import pallas as pl
from jax.experimental.pallas import tpu as pltpu
from jax.sharding import PartitionSpec as P

STEP = 2.0
HEAVY = 16.0
SQRT3 = math.sqrt(3.0)
SQRT5 = math.sqrt(5.0)
SQRT15 = math.sqrt(15.0)
F32 = jnp.float32
BF16 = jnp.bfloat16
I32 = jnp.int32
NT = (((1,), (1,)), ((), ()))
VM = pl.BlockSpec(memory_space=pltpu.VMEM)
SM = pl.BlockSpec(memory_space=pltpu.SMEM)
MESH = pl.DeviceIdType.MESH


def dot(a, b):
    return jnp.dot(a, b, preferred_element_type=F32)


def dot_nt(a, b):
    return lax.dot_general(a, b, NT, preferred_element_type=F32)


def split(x):
    hi = x.astype(BF16)
    return hi, (x - hi.astype(F32)).astype(BF16)


def halves(x):
    n = x.shape[0] // 2
    return x[:n] + x[n:]


def lane_take(tiles, idx):
    low = idx & 127
    high = idx >> 7
    out = jnp.take_along_axis(tiles[0], low, axis=1)
    for t in range(1, len(tiles)):
        out = jnp.where(high == t, jnp.take_along_axis(tiles[t], low, axis=1), out)
    return out


def spread(row, count=8):
    return jnp.broadcast_to(row, (count, row.shape[1]))


def build_hot(nbr, hot):
    @pl.loop(0, 8)
    def _(rc):
        at = pl.multiple_of(rc * 128, 128)
        ids = lax.broadcasted_iota(I32, (128, 128), 0) + at
        for it in range(4):
            for k in range(8):
                row = jnp.broadcast_to(nbr[k : k + 1, it * 128 : (it + 1) * 128], (128, 128))
                hot[it * 8 + k, pl.ds(at, 128), :] = jnp.where(ids == row, 1.0, 0.0).astype(BF16)


def energy_gradient(
    here, ext_own, ext_low, ext_up, nb_t, emb, r1, r2, mix1, mix2, rd1, rd2,
    to_low, to_up, to_low2, to_up2, kept,
    nb_s, geo, yy, bb, hot, m1, hs, ds1, gg, ww, m2, dg, dw, part, two, dh, dr, fl,
):
    for e in range(8):
        cols = slice(e * 128, (e + 1) * 128)
        ext = ext_low if e < 2 else (ext_own if e < 6 else ext_up)
        idx = nb_t[e]
        nb_s[:, cols] = idx
        fl[:, cols] = spread(ext_own[e][3:4])
        got = [lane_take([spread(x[c : c + 1]) for x in ext], idx) for c in range(4)]
        rx, ry, rz = [got[c] - spread(ext_own[e][c : c + 1]) for c in range(3)]
        s = jnp.sqrt(rx * rx + ry * ry + rz * rz + 1.0)
        inv = 1.0 / s
        ux, uy, uz = rx * inv, ry * inv, rz * inv
        for c, v in enumerate((ux, uy, uz, s, inv, got[3])):
            geo[c, :, cols] = v
        ys = (
            SQRT3 * ux, SQRT3 * uy, SQRT3 * uz,
            SQRT15 * ux * uy, SQRT15 * uy * uz,
            0.5 * SQRT5 * (2.0 * uz * uz - ux * ux - uy * uy),
            SQRT15 * ux * uz, 0.5 * SQRT15 * (ux * ux - uy * uy),
        )
        for l in range(8):
            yy[l, :, cols] = ys[l]
        for n in range(8):
            bb[n, :, cols] = jnp.exp(-0.5 * (s - (1.0 + n)) ** 2)

    w_rows = []
    for f in range(2):
        for n in range(8):
            w_rows.append(spread(r1[n : n + 1, :] * emb[f : f + 1, :] * 0.125))
    wt = jnp.concatenate(w_rows, axis=0)
    wth, wtl = split(wt)
    wh, wl = split(jnp.transpose(wt))
    zero = jnp.zeros((128, 128), BF16)
    wf = jnp.concatenate([jnp.concatenate([wh, wh], 1), jnp.concatenate([wl, zero], 1)], 0)
    wtf = jnp.concatenate([jnp.concatenate([wth, wth], 1), jnp.concatenate([wtl, zero], 1)], 0)
    r2s = r2[...] * 0.125
    rows = jnp.concatenate([emb[...], rd1[...], rd2[...], jnp.zeros((4, 128), F32), r2s], 0)
    colmat = jnp.transpose(jnp.concatenate([rows, jnp.zeros((112, 128), F32)], 0))
    e0, e1 = colmat[:, 0:1], colmat[:, 1:2]
    c_rd1, c_rd2 = colmat[:, 2:3], colmat[:, 3:4]
    m1h, m1l = split(mix1[...])
    m1s = jnp.concatenate([m1h, m1l], 0)
    m1t = jnp.transpose(mix1[...])
    m1th, m1tl = split(m1t)
    m1ts = jnp.concatenate([m1th, m1tl], 0)
    m2h, m2l = split(mix2[...])
    m2s = jnp.concatenate([m2h, m2l], 0)
    m2th, m2tl = split(jnp.transpose(mix2[...]))
    m2ts = jnp.concatenate([m2th, m2tl], 0)

    def mixed(ws, wh_, x):
        hi, lo = split(x)
        return halves(dot(ws, hi)) + dot(wh_, lo)

    @pl.loop(0, 4)
    def _(ch):
        sl = pl.ds(pl.multiple_of(ch * 256, 256), 256)
        f = geo[5, :, sl]
        bs = []
        for n in range(8):
            bs.append(bb[n, :, sl] * (1.0 - f))
        for n in range(8):
            bs.append(bb[n, :, sl] * f)
        q = [None, None, None]
        for l in range(9):
            z = jnp.concatenate(bs if l == 0 else [yy[l - 1, :, sl] * b for b in bs], 0)
            m = halves(dot(wf, jnp.concatenate(split(z), 0)))
            m1[l, :, sl] = m
            g = 0 if l == 0 else (1 if l < 4 else 2)
            q[g] = m * m if q[g] is None else q[g] + m * m
        v = mixed(m1s, m1h, jnp.concatenate(q, 0))
        sg = 1.0 / (1.0 + jnp.exp(-v))
        fc = fl[0:1, sl]
        h = e0 + fc * (e1 - e0) + v * sg
        ds1[:, sl] = sg * (1.0 + v * (1.0 - sg))
        hh = jnp.concatenate(split(h), 0)
        for o in range(2):
            hs[2 * ch + o] = hh[:, o * 128 : (o + 1) * 128]

    own_lanes = slice(256, 768)
    iota8 = lax.broadcasted_iota(I32, (8, 256), 0).astype(F32)
    r2th, r2tl = split(colmat[:, 8:16])
    r2lhs = jnp.concatenate([r2th.astype(F32), r2th.astype(F32), r2tl.astype(F32)], 1).astype(BF16)

    def own_at(it):
        return slice(256 + it * 128, 384 + it * 128)

    def basis(k, it):
        row = jnp.concatenate([geo[3, k : k + 1, own_at(it)], geo[3, k + 1 : k + 2, own_at(it)]], 1)
        off = spread(row) - 1.0 - iota8
        return off, jnp.exp(-0.5 * off * off)

    def gather(it, cc):
        at = it * 8 + 2 * cc
        feats = jnp.concatenate([hs[t] for t in range(8)], 1)
        got = halves(dot(feats, jnp.concatenate([hot[at], hot[at + 1]], 1)))
        _, bk = basis(2 * cc, it)
        bh, bl = split(bk)
        rhs = jnp.concatenate([bh.astype(F32), bl.astype(F32), bh.astype(F32)], 0).astype(BF16)
        wgt = dot(r2lhs, rhs)
        for o in range(2):
            gg[it, 2 * cc + o] = got[:, o * 128 : (o + 1) * 128]
            ww[it, 2 * cc + o] = wgt[:, o * 128 : (o + 1) * 128]

    def y_row(l, k, it):
        return yy[l - 1, k : k + 1, own_at(it)]

    def moments(it, cc):
        rows_ = slice(cc * 32, cc * 32 + 32)
        car = [gg[it, k, rows_] * ww[it, k, rows_] for k in range(8)]
        acc = car[0]
        for k in range(1, 8):
            acc = acc + car[k]
        m2[it, 0, rows_] = acc
        for l in range(1, 9):
            acc = y_row(l, 0, it) * car[0]
            for k in range(1, 8):
                acc = acc + y_row(l, k, it) * car[k]
            m2[it, l, rows_] = acc

    def middle(it):
        q = [None, None, None]
        for l in range(9):
            m = m2[it, l]
            g = 0 if l == 0 else (1 if l < 4 else 2)
            q[g] = m * m if q[g] is None else q[g] + m * m
        v = mixed(m2s, m2h, jnp.concatenate(q, 0))
        sg = 1.0 / (1.0 + jnp.exp(-v))
        dv = c_rd2 * (sg * (1.0 + v * (1.0 - sg)))
        dq = mixed(m2ts, m2th, dv) * 2.0
        for l in range(9):
            g = 0 if l == 0 else (1 if l < 4 else 2)
            m2[it, l] = m2[it, l] * dq[g * 128 : (g + 1) * 128]

    def backward(it, cc):
        rows_ = slice(cc * 32, cc * 32 + 32)
        rows_lo = slice(128 + cc * 32, 160 + cc * 32)
        lanes = slice(it * 128, (it + 1) * 128)
        dm = [m2[it, l, rows_] for l in range(9)]
        for k in range(8):
            g, w = gg[it, k, rows_], ww[it, k, rows_]
            car = g * w
            dcar = dm[0]
            for l in range(1, 9):
                dcar = dcar + y_row(l, k, it) * dm[l]
            for l in range(1, 9):
                pr = dm[l] * car
                pr = (pr[0:8] + pr[8:16]) + (pr[16:24] + pr[24:32])
                at8 = ((l - 1) * 8 + k) * 8
                part[at8 : at8 + 8, lanes] = pr if cc == 0 else part[at8 : at8 + 8, lanes] + pr
            hi, lo = split(dcar * w)
            dg[it * 8 + k, rows_] = hi
            dg[it * 8 + k, rows_lo] = lo
            hi, lo = split(dcar * g)
            dw[it * 8 + k, rows_] = hi
            dw[it * 8 + k, rows_lo] = lo

    def scatter(it, cc):
        cols = slice(cc * 256, (cc + 1) * 256)
        cot = jnp.concatenate([dg[it * 8 + k] for k in range(8)], 1)
        res = halves(dot_nt(cot, jnp.concatenate([hot[it * 8 + k, cols] for k in range(8)], 1)))
        dh[:, cols] = res if it == 0 else dh[:, cols] + res

    for cc in range(4):
        gather(0, cc)
    for it in range(4):

        @pl.when(here >= -it)
        def _():
            for cc in range(4):
                if it < 3:
                    gather(it + 1, cc)
                moments(it, cc)
            if it:
                scatter(it - 1, 0)
            middle(it)
            for cc in range(4):
                if it and cc:
                    scatter(it - 1, cc)
                backward(it, cc)

    for cc in range(4):
        scatter(3, cc)
    r2h, r2l = split(r2s)
    r2f = jnp.concatenate(
        [jnp.concatenate([r2h, r2h], 1).astype(F32), jnp.concatenate([r2l, jnp.zeros_like(r2l)], 1).astype(F32)], 0
    ).astype(BF16)
    for it in range(4):
        for cc in range(4):
            at = it * 8 + 2 * cc
            dbk = halves(dot(r2f, jnp.concatenate([dw[at], dw[at + 1]], 1)))
            off, bk = basis(2 * cc, it)
            res = -(dbk * bk * off)
            for o in range(2):
                at = 512 + (2 * cc + o) * 8
                part[at : at + 8, it * 128 : (it + 1) * 128] = res[:, o * 128 : (o + 1) * 128]
    sel = (lax.broadcasted_iota(I32, (72, 576), 1) >> 3) == lax.broadcasted_iota(I32, (72, 576), 0)
    sel = jnp.where(sel, 1.0, 0.0).astype(BF16)
    ph, pl_ = split(part[...])
    two[:, own_lanes] = dot(sel, ph) + dot(sel, pl_)

    @pl.loop(0, 4)
    def _(ch):
        sl = pl.ds(pl.multiple_of(ch * 256, 256), 256)
        is_own = jnp.where(jnp.logical_or(ch == 1, ch == 2), 1.0, 0.0).astype(F32)
        dv = (dh[:, sl] + c_rd1 * is_own) * ds1[:, sl]
        dq = mixed(m1ts, m1th, dv) * 2.0
        on = geo[5, :, sl] > 0.5
        ux, uy, uz = geo[0, :, sl], geo[1, :, sl], geo[2, :, sl]
        s, inv = geo[3, :, sl], geo[4, :, sl]
        bs = [bb[n, :, sl] for n in range(8)]
        dy, db = [None], [None] * 8
        for l in range(9):
            g = 0 if l == 0 else (1 if l < 4 else 2)
            dm = m1[l, :, sl] * dq[g * 128 : (g + 1) * 128]
            dz = halves(dot(wtf, jnp.concatenate(split(dm), 0)))
            y = None if l == 0 else yy[l - 1, :, sl]
            acc = None
            for n in range(8):
                t = jnp.where(on, dz[64 + n * 8 : 72 + n * 8], dz[n * 8 : n * 8 + 8])
                if l == 0:
                    db[n] = t
                else:
                    db[n] = db[n] + t * y
                    acc = t * bs[n] if acc is None else acc + t * bs[n]
            if l:
                dy.append(acc + two[(l - 1) * 8 : l * 8, sl])
        dsv = two[64:72, sl]
        for n in range(8):
            dsv = dsv - db[n] * bs[n] * (s - (1.0 + n))
        dux = SQRT3 * dy[1] + SQRT15 * (uy * dy[4] + uz * dy[7] + ux * dy[8]) - SQRT5 * ux * dy[6]
        duy = SQRT3 * dy[2] + SQRT15 * (ux * dy[4] + uz * dy[5] - uy * dy[8]) - SQRT5 * uy * dy[6]
        duz = SQRT3 * dy[3] + SQRT15 * (uy * dy[5] + ux * dy[7]) + 2.0 * SQRT5 * uz * dy[6]
        along = dsv - (dux * ux + duy * uy + duz * uz) * inv
        dr[0, :, sl] = dux * inv + ux * along
        dr[1, :, sl] = duy * inv + uy * along
        dr[2, :, sl] = duz * inv + uz * along

    tile_ids = lax.broadcasted_iota(I32, (8, 1024), 0)
    lane_ids = lax.broadcasted_iota(I32, (128, 1024), 0)

    def onto(index_row, values):
        there = spread(index_row >> 7) == tile_ids
        his, los = [], []
        for v in values:
            m = jnp.where(there, spread(v), 0.0)
            hi = m.astype(BF16).astype(F32)
            his.append(hi)
            los.append(m - hi)
        lhs = jnp.concatenate(his + los, 0).astype(BF16)
        rhs = jnp.where(jnp.broadcast_to(index_row & 127, (128, 1024)) == lane_ids, 1.0, 0.0).astype(BF16)
        return lhs, rhs

    selfs = lax.broadcasted_iota(I32, (1, 1024), 1)
    lhs, rhs = onto(selfs, [-jnp.sum(dr[c], axis=0, keepdims=True) for c in range(3)])
    acc_own = dot_nt(lhs, rhs)
    acc_low = jnp.zeros((48, 128), F32)
    acc_up = jnp.zeros((48, 128), F32)
    for k in range(8):
        lhs, rhs = onto(nb_s[k : k + 1, :], [dr[c, k : k + 1, :] for c in range(3)])
        acc_own = acc_own + dot_nt(lhs[:, 256:768], rhs[:, 256:768])
        acc_low = acc_low + dot_nt(lhs[:, :256], rhs[:, :256])
        acc_up = acc_up + dot_nt(lhs[:, 768:], rhs[:, 768:])
    acc_own, acc_low, acc_up = halves(acc_own), halves(acc_low), halves(acc_up)

    def put(ref, at, acc, c, first, count):
        ref[at : at + count, :] = acc[c * 8 + first : c * 8 + first + count, :]

    for c in range(3):
        put(kept, c * 4, acc_own, c, 2, 4)
        put(kept, 12 + c * 4, acc_low, c, 6, 2)
        put(kept, 14 + c * 4, acc_up, c, 0, 2)
        put(to_low, c * 4, acc_low, c, 2, 4)
        put(to_low, 12 + c * 2, acc_own, c, 0, 2)
        put(to_up, c * 4, acc_up, c, 2, 4)
        put(to_up, 12 + c * 2, acc_own, c, 6, 2)
        put(to_low2, c * 2, acc_low, c, 0, 2)
        put(to_up2, c * 2, acc_up, c, 6, 2)
    pad2, pad6 = jnp.zeros((2, 128), F32), jnp.zeros((6, 128), F32)
    to_low[18:24, :] = pad6
    to_up[18:24, :] = pad6
    to_low2[6:8, :] = pad2
    to_up2[6:8, :] = pad2


COMPUTE_SCRATCH = [
    pltpu.VMEM((8, 1024), I32),
    pltpu.VMEM((6, 8, 1024), F32),
    pltpu.VMEM((8, 8, 1024), F32),
    pltpu.VMEM((8, 8, 1024), F32),
    pltpu.VMEM((32, 1024, 128), BF16),
    pltpu.VMEM((9, 128, 1024), F32),
    pltpu.VMEM((8, 256, 128), BF16),
    pltpu.VMEM((128, 1024), F32),
    pltpu.VMEM((4, 8, 128, 128), F32),
    pltpu.VMEM((4, 8, 128, 128), F32),
    pltpu.VMEM((4, 9, 128, 128), F32),
    pltpu.VMEM((32, 256, 128), BF16),
    pltpu.VMEM((32, 256, 128), BF16),
    pltpu.VMEM((576, 512), F32),
    pltpu.VMEM((72, 1024), F32),
    pltpu.VMEM((128, 1024), F32),
    pltpu.VMEM((3, 8, 1024), F32),
    pltpu.VMEM((8, 1024), F32),
]


def ring_tables(beads):
    b = np.arange(beads, dtype=np.float64)
    angle = beads * np.sin(np.pi * b / beads)
    safe = np.where(b == 0, 1.0, angle)
    reach = np.where(b == 0, STEP, STEP * np.sin(angle) / safe)
    stiff = angle * np.sin(angle) / STEP
    phase = np.cos(2.0 * np.pi * np.outer(b, b) / beads) / beads
    return [(phase @ f).tolist() for f in (np.cos(angle), reach, stiff)]


def rows12(ref):
    return jnp.concatenate([ref[c, 0:1, t * 128 : (t + 1) * 128] for c in range(3) for t in range(4)], 0)


def step_kernel(
    domains, beads,
    pos, mom, spec, nbr, send_ref, emb, r1, r2, mix1, mix2, rd1, rd2,
    new_pos, new_mom,
    msg_up, msg_low, in_low, in_up, in_low2, in_up2,
    to_low, to_up, to_low2, to_up2, kept,
    from_low, from_up, from_low2, from_up2, q_src, p_src, q_all, p_all,
    fs_sem, fr_sem, hs_sem, hr_sem, qs_sem, qr_sem, ps_sem, pr_sem,
    *work,
):
    me = lax.axis_index("space")
    bead = lax.axis_index("bead")
    near = [lax.rem(me + s + domains, domains) for s in (1, -1, 2, -2)]
    ring = [lax.rem(bead + o, beads) for o in range(beads)]
    barrier = pltpu.get_barrier_semaphore()
    for p in near:
        pl.semaphore_signal(barrier, inc=1, device_id={"space": p}, device_id_type=MESH)
    for o in range(1, beads):
        pl.semaphore_signal(barrier, inc=1, device_id={"bead": ring[o]}, device_id_type=MESH)

    flags = spec[...].astype(F32)
    send = send_ref[...]
    own_t, nbr_t = [], []
    for t in range(4):
        lanes = slice(t * 128, (t + 1) * 128)
        quad = [pos[c, 0:1, lanes] for c in range(3)] + [flags[:, lanes]]
        own_t.append(jnp.concatenate(quad + quad, 0))
        nbr_t.append(nbr[:, lanes])

    def sent(tiles, half):
        return [
            lane_take(tiles, spread(send[:, at : at + 128])) for at in (half * 256, half * 256 + 128)
        ]

    def pair(x, y):
        return jnp.concatenate([x[0:4], y[4:8]], 0)

    def both(x):
        return [jnp.concatenate([x[0:4], x[0:4]], 0), jnp.concatenate([x[4:8], x[4:8]], 0)]

    ghosts = [sent(own_t, 0), sent(own_t, 1)]
    q_src[...] = rows12(pos)
    for msg, half in ((msg_low, 0), (msg_up, 1)):
        lists = sent(nbr_t, half)
        msg[0:8, :] = pair(own_t[0], own_t[1])
        msg[8:16, :] = pair(own_t[2], own_t[3])
        msg[16:24, :] = pair(*ghosts[half])
        msg[24:32, :] = lists[0].astype(F32)
        msg[32:40, :] = lists[1].astype(F32)
    pl.semaphore_wait(barrier, 4 + beads - 1)

    def to_near(srcs, dsts, s_sem, r_sem):
        out = []
        for i, (p, s, dst) in enumerate(zip(near, srcs, dsts)):
            c = pltpu.make_async_remote_copy(
                src_ref=s, dst_ref=dst, send_sem=s_sem.at[i], recv_sem=r_sem.at[i],
                device_id={"space": p}, device_id_type=MESH,
            )
            c.start()
            out.append(c)
        return out

    def share(src, dst, s_sem, r_sem):
        out = []
        for o in range(1, beads):
            c = pltpu.make_async_remote_copy(
                src_ref=src, dst_ref=dst.at[o], send_sem=s_sem.at[o], recv_sem=r_sem.at[o],
                device_id={"bead": ring[o]}, device_id_type=MESH,
            )
            c.start()
            out.append(c)
        return out

    halo = to_near(
        (msg_up, msg_low, msg_up.at[16:24], msg_low.at[16:24]), (in_low, in_up, in_low2, in_up2), fs_sem, fr_sem
    )
    build_hot(nbr, work[4])
    two = work[14]
    two[...] = jnp.zeros_like(two)
    for c in halo:
        c.wait()
    q_copies = share(q_src, q_all, qs_sem, qr_sem)

    def whole(ref):
        return both(ref[0:8, :]) + both(ref[8:16, :])

    ext_own = both(in_low[16:24, :]) + own_t + both(in_up[16:24, :])
    ext_low = both(in_low2[...]) + whole(in_low) + ghosts[0]
    ext_up = ghosts[1] + whole(in_up) + both(in_up2[...])
    nb_t = [in_low[24:32, :].astype(I32), in_low[32:40, :].astype(I32)] + nbr_t
    nb_t = nb_t + [in_up[24:32, :].astype(I32), in_up[32:40, :].astype(I32)]
    energy_gradient(
        me, ext_own, ext_low, ext_up, nb_t, emb, r1, r2, mix1, mix2, rd1, rd2,
        to_low, to_up, to_low2, to_up2, kept, *work,
    )
    copies = to_near(
        (to_up, to_low, to_up2, to_low2), (from_low, from_up, from_low2, from_up2), hs_sem, hr_sem
    )

    there = [spread(send[:, t * 128 : (t + 1) * 128] >> 7) for t in range(4)]
    iota8 = lax.broadcasted_iota(I32, (8, 128), 0)
    rhs = jnp.where(
        jnp.broadcast_to(send & 127, (128, 512)) == lax.broadcasted_iota(I32, (128, 512), 0), 1.0, 0.0
    ).astype(BF16)
    mass4 = HEAVY - (HEAVY - 1.0) * jnp.concatenate(
        [flags[:, t * 128 : (t + 1) * 128] for t in range(4)], 0
    )
    mass = jnp.concatenate([mass4, mass4, mass4], 0)
    p12 = rows12(mom)
    for c in copies:
        c.wait()

    his, los = [], []
    for c in range(3):
        parts = []
        for t in range(4):
            near_, far = (from_low, from_low2) if t < 2 else (from_up, from_up2)
            at, a12, a2 = 12 + c * 4 + t, 12 + c * 2 + t % 2, c * 2 + t % 2
            v = kept[at : at + 1, :] + near_[a12 : a12 + 1, :] + far[a2 : a2 + 1, :]
            parts.append(jnp.where(there[t] == iota8, spread(v), 0.0))
        m = jnp.concatenate(parts, 1)
        hi = m.astype(BF16).astype(F32)
        his.append(hi)
        los.append(m - hi)
    got = halves(dot_nt(jnp.concatenate(his + los, 0).astype(BF16), rhs))
    got = jnp.concatenate([got[c * 8 : c * 8 + 4] for c in range(3)], 0)
    kicked = p12 - (kept[0:12, :] + from_low[0:12, :] + from_up[0:12, :] + got)
    p_src[...] = kicked
    p_copies = share(p_src, p_all, ps_sem, pr_sem)

    turn, reach, stiff = ring_tables(beads)
    q = q_src[...]
    qa, qs = turn[0] * q, stiff[0] * q
    for o, c in zip(range(1, beads), q_copies):
        c.wait()
        q = q_all[o]
        qa, qs = qa + turn[o] * q, qs + stiff[o] * q
    pa, pr = turn[0] * kicked, reach[0] * kicked
    for o, c in zip(range(1, beads), p_copies):
        c.wait()
        p = p_all[o]
        pa, pr = pa + turn[o] * p, pr + reach[o] * p
    qn = qa + pr / mass
    pn = pa - mass * qs
    for c in range(3):
        for t in range(4):
            at = c * 4 + t
            new_pos[c, 0:1, t * 128 : (t + 1) * 128] = qn[at : at + 1]
            new_mom[c, 0:1, t * 128 : (t + 1) * 128] = pn[at : at + 1]


def shards(
    positions, momenta, species, neighbours, send_list, embedding,
    radial_one, radial_two, mix_one, mix_two, read_one, read_two,
):
    domains, beads = lax.axis_size("space"), lax.axis_size("bead")
    dma = lambda n: pltpu.SemaphoreType.DMA((n,))
    rows = lambda n: pltpu.VMEM((n, 128), F32)
    q, p = pl.pallas_call(
        lambda *refs: step_kernel(domains, beads, *refs),
        out_shape=(jax.ShapeDtypeStruct((3, 1, 512), F32),) * 2,
        in_specs=[VM] * 12,
        out_specs=(VM,) * 2,
        scratch_shapes=[rows(n) for n in (40, 40, 40, 40, 8, 8, 24, 24, 8, 8, 24, 24, 24, 8, 8, 12, 12)]
        + [pltpu.VMEM((beads, 12, 128), F32)] * 2
        + [dma(4)] * 4 + [dma(beads)] * 4 + COMPUTE_SCRATCH,
        compiler_params=pltpu.CompilerParams(
            collective_id=0, has_side_effects=True, vmem_limit_bytes=60 << 20
        ),
        name="md_step",
    )(
        jnp.transpose(positions, (1, 0, 2)), jnp.transpose(momenta, (1, 0, 2)), species[None], neighbours,
        send_list[None], embedding, radial_one, radial_two, mix_one, mix_two, read_one[None], read_two[None],
    )
    return jnp.transpose(q, (1, 0, 2)), jnp.transpose(p, (1, 0, 2))


def solution(mesh):
    beads = P("bead", None, "space")
    placed = (beads, beads, P("space"), P(None, "space"), P("space")) + (P(),) * 7
    return jax.shard_map(shards, mesh=mesh, in_specs=placed, out_specs=(beads, beads), check_vma=False)
```

```python
import math

import numpy as np

import jax
import jax.numpy as jnp
from jax import lax
from jax.experimental import pallas as pl
from jax.experimental.pallas import tpu as pltpu
from jax.sharding import PartitionSpec as P

STEP = 2.0
HEAVY = 16.0
SQRT3 = math.sqrt(3.0)
SQRT5 = math.sqrt(5.0)
SQRT15 = math.sqrt(15.0)
F32 = jnp.float32
BF16 = jnp.bfloat16
I32 = jnp.int32
NT = (((1,), (1,)), ((), ()))
VM = pl.BlockSpec(memory_space=pltpu.VMEM)
SM = pl.BlockSpec(memory_space=pltpu.SMEM)
MESH = pl.DeviceIdType.MESH


def dot(a, b):
    return jnp.dot(a, b, preferred_element_type=F32)


def dot_nt(a, b):
    return lax.dot_general(a, b, NT, preferred_element_type=F32)


def split(x):
    hi = x.astype(BF16)
    return hi, (x - hi.astype(F32)).astype(BF16)


def halves(x):
    n = x.shape[0] // 2
    return x[:n] + x[n:]


def lane_take(tiles, idx):
    low = idx & 127
    high = idx >> 7
    out = jnp.take_along_axis(tiles[0], low, axis=1)
    for t in range(1, len(tiles)):
        out = jnp.where(high == t, jnp.take_along_axis(tiles[t], low, axis=1), out)
    return out


def spread(row, count=8):
    return jnp.broadcast_to(row, (count, row.shape[1]))


def build_hot(nbr, hot):
    @pl.loop(0, 8)
    def _(rc):
        at = pl.multiple_of(rc * 128, 128)
        ids = lax.broadcasted_iota(I32, (128, 128), 0) + at
        for it in range(4):
            for k in range(8):
                row = jnp.broadcast_to(nbr[k : k + 1, it * 128 : (it + 1) * 128], (128, 128))
                hot[it * 8 + k, pl.ds(at, 128), :] = jnp.where(ids == row, 1.0, 0.0).astype(BF16)


def prepare(nbr, weights, work):
    emb, r1, r2, mix1, mix2, rd1, rd2 = weights
    hot, two, lam = work[4], work[14], work[18]
    build_hot(nbr, hot)
    two[...] = jnp.zeros_like(two)
    lane_ids = lax.broadcasted_iota(I32, (128, 512), 0)
    for k in range(8):
        row = jnp.broadcast_to(nbr[k : k + 1, :] & 127, (128, 512))
        one = jnp.where(row == lane_ids, 1.0, 0.0).astype(BF16)
        for t in range(4):
            lam[k * 4 + t] = one[:, t * 128 : (t + 1) * 128]
    w_rows = []
    for f in range(2):
        for n in range(8):
            w_rows.append(spread(r1[n : n + 1, :] * emb[f : f + 1, :] * 0.125))
    wt = jnp.concatenate(w_rows, axis=0)
    wth, wtl = split(wt)
    wh, wl = split(jnp.transpose(wt))
    zero = jnp.zeros((128, 128), BF16)
    wf = jnp.concatenate([jnp.concatenate([wh, wh], 1), jnp.concatenate([wl, zero], 1)], 0)
    wtf = jnp.concatenate([jnp.concatenate([wth, wth], 1), jnp.concatenate([wtl, zero], 1)], 0)
    r2s = r2[...] * 0.125
    rows = jnp.concatenate([emb[...], rd1[...], rd2[...], jnp.zeros((4, 128), F32), r2s], 0)
    colmat = jnp.transpose(jnp.concatenate([rows, jnp.zeros((112, 128), F32)], 0))
    e0, e1 = colmat[:, 0:1], colmat[:, 1:2]
    c_rd1, c_rd2 = colmat[:, 2:3], colmat[:, 3:4]
    m1h, m1l = split(mix1[...])
    m1s = jnp.concatenate([m1h, m1l], 0)
    m1t = jnp.transpose(mix1[...])
    m1th, m1tl = split(m1t)
    m1ts = jnp.concatenate([m1th, m1tl], 0)
    m2h, m2l = split(mix2[...])
    m2s = jnp.concatenate([m2h, m2l], 0)
    m2th, m2tl = split(jnp.transpose(mix2[...]))
    m2ts = jnp.concatenate([m2th, m2tl], 0)
    r2th, r2tl = split(colmat[:, 8:16])
    r2lhs = jnp.concatenate([r2th.astype(F32), r2th.astype(F32), r2tl.astype(F32)], 1).astype(BF16)
    r2h, r2l = split(r2s)
    r2f = jnp.concatenate(
        [jnp.concatenate([r2h, r2h], 1).astype(F32), jnp.concatenate([r2l, jnp.zeros_like(r2l)], 1).astype(F32)], 0
    ).astype(BF16)
    return wf, wtf, e0, e1, c_rd1, c_rd2, m1h, m1s, m1th, m1ts, m2h, m2s, m2th, m2ts, r2s, r2lhs, r2f


def energy_gradient(
    prepared, ext_own, ext_low, ext_up, nb_t,
    to_low, to_up, to_low2, to_up2, kept,
    nb_s, geo, yy, bb, hot, m1, hs, ds1, gg, ww, m2, dg, dw, part, two, dh, dr, fl, lam,
):
    (wf, wtf, e0, e1, c_rd1, c_rd2, m1h, m1s, m1th, m1ts, m2h, m2s, m2th, m2ts, r2s, r2lhs, r2f) = prepared
    for e in range(8):
        cols = slice(e * 128, (e + 1) * 128)
        ext = ext_low if e < 2 else (ext_own if e < 6 else ext_up)
        idx = nb_t[e]
        nb_s[:, cols] = idx
        fl[:, cols] = spread(ext_own[e][3:4])
        got = [lane_take([spread(x[c : c + 1]) for x in ext], idx) for c in range(4)]
        rx, ry, rz = [got[c] - spread(ext_own[e][c : c + 1]) for c in range(3)]
        s = jnp.sqrt(rx * rx + ry * ry + rz * rz + 1.0)
        inv = 1.0 / s
        ux, uy, uz = rx * inv, ry * inv, rz * inv
        for c, v in enumerate((ux, uy, uz, s, inv, got[3])):
            geo[c, :, cols] = v
        ys = (
            SQRT3 * ux, SQRT3 * uy, SQRT3 * uz,
            SQRT15 * ux * uy, SQRT15 * uy * uz,
            0.5 * SQRT5 * (2.0 * uz * uz - ux * ux - uy * uy),
            SQRT15 * ux * uz, 0.5 * SQRT15 * (ux * ux - uy * uy),
        )
        for l in range(8):
            yy[l, :, cols] = ys[l]
        for n in range(8):
            bb[n, :, cols] = jnp.exp(-0.5 * (s - (1.0 + n)) ** 2)

    def mixed(ws, wh_, x):
        hi, lo = split(x)
        return halves(dot(ws, hi)) + dot(wh_, lo)

    @pl.loop(0, 4, unroll=2)
    def _(ch):
        sl = pl.ds(pl.multiple_of(ch * 256, 256), 256)
        f = geo[5, :, sl]
        bs = []
        for n in range(8):
            bs.append(bb[n, :, sl] * (1.0 - f))
        for n in range(8):
            bs.append(bb[n, :, sl] * f)
        q = [None, None, None]
        for l in range(9):
            z = jnp.concatenate(bs if l == 0 else [yy[l - 1, :, sl] * b for b in bs], 0)
            m = halves(dot(wf, jnp.concatenate(split(z), 0)))
            m1[l, :, sl] = m
            g = 0 if l == 0 else (1 if l < 4 else 2)
            q[g] = m * m if q[g] is None else q[g] + m * m
        v = mixed(m1s, m1h, jnp.concatenate(q, 0))
        sg = 1.0 / (1.0 + jnp.exp(-v))
        fc = fl[0:1, sl]
        h = e0 + fc * (e1 - e0) + v * sg
        ds1[:, sl] = sg * (1.0 + v * (1.0 - sg))
        hh = jnp.concatenate(split(h), 0)
        for o in range(2):
            hs[2 * ch + o] = hh[:, o * 128 : (o + 1) * 128]

    own_lanes = slice(256, 768)
    iota8 = lax.broadcasted_iota(I32, (8, 256), 0).astype(F32)

    def own_at(it):
        return slice(256 + it * 128, 384 + it * 128)

    def basis(k, it):
        row = jnp.concatenate([geo[3, k : k + 1, own_at(it)], geo[3, k + 1 : k + 2, own_at(it)]], 1)
        off = spread(row) - 1.0 - iota8
        return off, jnp.exp(-0.5 * off * off)

    def gather(it, cc):
        at = it * 8 + 2 * cc
        feats = jnp.concatenate([hs[t] for t in range(8)], 1)
        got = halves(dot(feats, jnp.concatenate([hot[at], hot[at + 1]], 1)))
        _, bk = basis(2 * cc, it)
        bh, bl = split(bk)
        rhs = jnp.concatenate([bh.astype(F32), bl.astype(F32), bh.astype(F32)], 0).astype(BF16)
        wgt = dot(r2lhs, rhs)
        for o in range(2):
            gg[it, 2 * cc + o] = got[:, o * 128 : (o + 1) * 128]
            ww[it, 2 * cc + o] = wgt[:, o * 128 : (o + 1) * 128]

    def y_row(l, k, it):
        return yy[l - 1, k : k + 1, own_at(it)]

    def moments(it, cc):
        rows_ = slice(cc * 32, cc * 32 + 32)
        car = [gg[it, k, rows_] * ww[it, k, rows_] for k in range(8)]
        acc = car[0]
        for k in range(1, 8):
            acc = acc + car[k]
        m2[it, 0, rows_] = acc
        for l in range(1, 9):
            acc = y_row(l, 0, it) * car[0]
            for k in range(1, 8):
                acc = acc + y_row(l, k, it) * car[k]
            m2[it, l, rows_] = acc

    def middle(it):
        q = [None, None, None]
        for l in range(9):
            m = m2[it, l]
            g = 0 if l == 0 else (1 if l < 4 else 2)
            q[g] = m * m if q[g] is None else q[g] + m * m
        v = mixed(m2s, m2h, jnp.concatenate(q, 0))
        sg = 1.0 / (1.0 + jnp.exp(-v))
        dv = c_rd2 * (sg * (1.0 + v * (1.0 - sg)))
        dq = mixed(m2ts, m2th, dv) * 2.0
        for l in range(9):
            g = 0 if l == 0 else (1 if l < 4 else 2)
            m2[it, l] = m2[it, l] * dq[g * 128 : (g + 1) * 128]

    def backward(it, cc):
        rows_ = slice(cc * 32, cc * 32 + 32)
        rows_lo = slice(128 + cc * 32, 160 + cc * 32)
        lanes = slice(it * 128, (it + 1) * 128)
        dm = [m2[it, l, rows_] for l in range(9)]
        for k in range(8):
            g, w = gg[it, k, rows_], ww[it, k, rows_]
            car = g * w
            dcar = dm[0]
            for l in range(1, 9):
                dcar = dcar + y_row(l, k, it) * dm[l]
            for l in range(1, 9):
                pr = dm[l] * car
                pr = (pr[0:8] + pr[8:16]) + (pr[16:24] + pr[24:32])
                at8 = ((l - 1) * 8 + k) * 8
                part[at8 : at8 + 8, lanes] = pr if cc == 0 else part[at8 : at8 + 8, lanes] + pr
            hi, lo = split(dcar * w)
            dg[it * 8 + k, rows_] = hi
            dg[it * 8 + k, rows_lo] = lo
            hi, lo = split(dcar * g)
            dw[it * 8 + k, rows_] = hi
            dw[it * 8 + k, rows_lo] = lo

    def scatter(it, cc):
        cols = slice(cc * 256, (cc + 1) * 256)
        cot = jnp.concatenate([dg[it * 8 + k] for k in range(8)], 1)
        res = halves(dot_nt(cot, jnp.concatenate([hot[it * 8 + k, cols] for k in range(8)], 1)))
        dh[:, cols] = res if it == 0 else dh[:, cols] + res

    for cc in range(4):
        gather(0, cc)
    for it in range(4):
        for cc in range(4):
            if it < 3:
                gather(it + 1, cc)
            moments(it, cc)
    for it in range(4):
        middle(it)
    for it in range(4):
        for cc in range(4):
            if it:
                scatter(it - 1, cc)
            backward(it, cc)
    for cc in range(4):
        scatter(3, cc)
    for it in range(4):
        for cc in range(4):
            at = it * 8 + 2 * cc
            dbk = halves(dot(r2f, jnp.concatenate([dw[at], dw[at + 1]], 1)))
            off, bk = basis(2 * cc, it)
            res = -(dbk * bk * off)
            for o in range(2):
                at = 512 + (2 * cc + o) * 8
                part[at : at + 8, it * 128 : (it + 1) * 128] = res[:, o * 128 : (o + 1) * 128]
    sel = (lax.broadcasted_iota(I32, (72, 576), 1) >> 3) == lax.broadcasted_iota(I32, (72, 576), 0)
    sel = jnp.where(sel, 1.0, 0.0).astype(BF16)
    ph, pl_ = split(part[...])
    two[:, own_lanes] = dot(sel, ph) + dot(sel, pl_)

    @pl.loop(0, 4, unroll=2)
    def _(ch):
        sl = pl.ds(pl.multiple_of(ch * 256, 256), 256)
        is_own = jnp.where(jnp.logical_or(ch == 1, ch == 2), 1.0, 0.0).astype(F32)
        dv = (dh[:, sl] + c_rd1 * is_own) * ds1[:, sl]
        dq = mixed(m1ts, m1th, dv) * 2.0
        on = geo[5, :, sl] > 0.5
        ux, uy, uz = geo[0, :, sl], geo[1, :, sl], geo[2, :, sl]
        s, inv = geo[3, :, sl], geo[4, :, sl]
        bs = [bb[n, :, sl] for n in range(8)]
        dy, db = [None], [None] * 8
        for l in range(9):
            g = 0 if l == 0 else (1 if l < 4 else 2)
            dm = m1[l, :, sl] * dq[g * 128 : (g + 1) * 128]
            dz = halves(dot(wtf, jnp.concatenate(split(dm), 0)))
            y = None if l == 0 else yy[l - 1, :, sl]
            acc = None
            for n in range(8):
                t = jnp.where(on, dz[64 + n * 8 : 72 + n * 8], dz[n * 8 : n * 8 + 8])
                if l == 0:
                    db[n] = t
                else:
                    db[n] = db[n] + t * y
                    acc = t * bs[n] if acc is None else acc + t * bs[n]
            if l:
                dy.append(acc + two[(l - 1) * 8 : l * 8, sl])
        dsv = two[64:72, sl]
        for n in range(8):
            dsv = dsv - db[n] * bs[n] * (s - (1.0 + n))
        dux = SQRT3 * dy[1] + SQRT15 * (uy * dy[4] + uz * dy[7] + ux * dy[8]) - SQRT5 * ux * dy[6]
        duy = SQRT3 * dy[2] + SQRT15 * (ux * dy[4] + uz * dy[5] - uy * dy[8]) - SQRT5 * uy * dy[6]
        duz = SQRT3 * dy[3] + SQRT15 * (uy * dy[5] + ux * dy[7]) + 2.0 * SQRT5 * uz * dy[6]
        along = dsv - (dux * ux + duy * uy + duz * uz) * inv
        dr[0, :, sl] = dux * inv + ux * along
        dr[1, :, sl] = duy * inv + uy * along
        dr[2, :, sl] = duz * inv + uz * along

    tile_ids = lax.broadcasted_iota(I32, (8, 1024), 0)
    lane_ids = lax.broadcasted_iota(I32, (128, 256), 0)
    acc_own = jnp.zeros((48, 128), F32)
    acc_low = jnp.zeros((48, 128), F32)
    acc_up = jnp.zeros((48, 128), F32)
    for k in range(8):
        row = nb_s[k : k + 1, :]
        there = spread(row >> 7) == tile_ids
        his, los = [], []
        for c in range(3):
            m = jnp.where(there, spread(dr[c, k : k + 1, :]), 0.0)
            hi = m.astype(BF16).astype(F32)
            his.append(hi)
            los.append(m - hi)
        lhs = jnp.concatenate(his + los, 0).astype(BF16)

        def ghost(first):
            part_ = jnp.broadcast_to(row[:, first : first + 256] & 127, (128, 256))
            return jnp.where(part_ == lane_ids, 1.0, 0.0).astype(BF16)

        own_hot = jnp.concatenate([lam[k * 4 + t] for t in range(4)], 1)
        acc_own = acc_own + dot_nt(lhs[:, 256:768], own_hot)
        acc_low = acc_low + dot_nt(lhs[:, :256], ghost(0))
        acc_up = acc_up + dot_nt(lhs[:, 768:], ghost(768))
    selfs = [jnp.sum(dr[c], axis=0, keepdims=True) for c in range(3)]
    selfs = jnp.concatenate([v[:, t * 128 : (t + 1) * 128] for v in selfs for t in range(8)], 0)
    acc_own, acc_low, acc_up = halves(acc_own) - selfs, halves(acc_low), halves(acc_up)

    def put(ref, at, acc, c, first, count):
        ref[at : at + count, :] = acc[c * 8 + first : c * 8 + first + count, :]

    for c in range(3):
        put(kept, c * 4, acc_own, c, 2, 4)
        put(kept, 12 + c * 4, acc_low, c, 6, 2)
        put(kept, 14 + c * 4, acc_up, c, 0, 2)
        put(to_low, c * 4, acc_low, c, 2, 4)
        put(to_low, 12 + c * 2, acc_own, c, 0, 2)
        put(to_up, c * 4, acc_up, c, 2, 4)
        put(to_up, 12 + c * 2, acc_own, c, 6, 2)
        put(to_low2, c * 2, acc_low, c, 0, 2)
        put(to_up2, c * 2, acc_up, c, 6, 2)
    pad2, pad6 = jnp.zeros((2, 128), F32), jnp.zeros((6, 128), F32)
    to_low[18:24, :] = pad6
    to_up[18:24, :] = pad6
    to_low2[6:8, :] = pad2
    to_up2[6:8, :] = pad2


COMPUTE_SCRATCH = [
    pltpu.VMEM((8, 1024), I32),
    pltpu.VMEM((6, 8, 1024), F32),
    pltpu.VMEM((8, 8, 1024), F32),
    pltpu.VMEM((8, 8, 1024), F32),
    pltpu.VMEM((32, 1024, 128), BF16),
    pltpu.VMEM((9, 128, 1024), F32),
    pltpu.VMEM((8, 256, 128), BF16),
    pltpu.VMEM((128, 1024), F32),
    pltpu.VMEM((4, 8, 128, 128), F32),
    pltpu.VMEM((4, 8, 128, 128), F32),
    pltpu.VMEM((4, 9, 128, 128), F32),
    pltpu.VMEM((32, 256, 128), BF16),
    pltpu.VMEM((32, 256, 128), BF16),
    pltpu.VMEM((576, 512), F32),
    pltpu.VMEM((72, 1024), F32),
    pltpu.VMEM((128, 1024), F32),
    pltpu.VMEM((3, 8, 1024), F32),
    pltpu.VMEM((8, 1024), F32),
    pltpu.VMEM((32, 128, 128), BF16),
]


def ring_tables(beads):
    b = np.arange(beads, dtype=np.float64)
    angle = beads * np.sin(np.pi * b / beads)
    safe = np.where(b == 0, 1.0, angle)
    reach = np.where(b == 0, STEP, STEP * np.sin(angle) / safe)
    stiff = angle * np.sin(angle) / STEP
    phase = np.cos(2.0 * np.pi * np.outer(b, b) / beads) / beads
    return [(phase @ f).tolist() for f in (np.cos(angle), reach, stiff)]


def rows12(ref):
    return jnp.concatenate([ref[c, 0:1, t * 128 : (t + 1) * 128] for c in range(3) for t in range(4)], 0)


def step_kernel(
    domains, beads,
    pos, mom, spec, nbr, send_ref, emb, r1, r2, mix1, mix2, rd1, rd2,
    new_pos, new_mom,
    msg_up, msg_low, in_low, in_up, in_low2, in_up2,
    to_low, to_up, to_low2, to_up2, kept,
    from_low, from_up, from_low2, from_up2, q_src, p_src, q_all, p_all,
    fs_sem, fr_sem, hs_sem, hr_sem, qs_sem, qr_sem, ps_sem, pr_sem,
    *work,
):
    me = lax.axis_index("space")
    bead = lax.axis_index("bead")
    near = [lax.rem(me + s + domains, domains) for s in (1, -1, 2, -2)]
    ring = [lax.rem(bead + o, beads) for o in range(beads)]
    barrier = pltpu.get_barrier_semaphore()
    for p in near:
        pl.semaphore_signal(barrier, inc=1, device_id={"space": p}, device_id_type=MESH)
    for o in range(1, beads):
        pl.semaphore_signal(barrier, inc=1, device_id={"bead": ring[o]}, device_id_type=MESH)

    flags = spec[...].astype(F32)
    send = send_ref[...]
    own_t, nbr_t = [], []
    for t in range(4):
        lanes = slice(t * 128, (t + 1) * 128)
        quad = [pos[c, 0:1, lanes] for c in range(3)] + [flags[:, lanes]]
        own_t.append(jnp.concatenate(quad + quad, 0))
        nbr_t.append(nbr[:, lanes])

    def sent(tiles, half):
        return [
            lane_take(tiles, spread(send[:, at : at + 128])) for at in (half * 256, half * 256 + 128)
        ]

    def pair(x, y):
        return jnp.concatenate([x[0:4], y[4:8]], 0)

    def both(x):
        return [jnp.concatenate([x[0:4], x[0:4]], 0), jnp.concatenate([x[4:8], x[4:8]], 0)]

    ghosts = [sent(own_t, 0), sent(own_t, 1)]
    q_src[...] = rows12(pos)
    for msg, half in ((msg_low, 0), (msg_up, 1)):
        lists = sent(nbr_t, half)
        msg[0:8, :] = pair(own_t[0], own_t[1])
        msg[8:16, :] = pair(own_t[2], own_t[3])
        msg[16:24, :] = pair(*ghosts[half])
        msg[24:32, :] = lists[0].astype(F32)
        msg[32:40, :] = lists[1].astype(F32)
    pl.semaphore_wait(barrier, 4 + beads - 1)

    def to_near(srcs, dsts, s_sem, r_sem):
        out = []
        for i, (p, s, dst) in enumerate(zip(near, srcs, dsts)):
            c = pltpu.make_async_remote_copy(
                src_ref=s, dst_ref=dst, send_sem=s_sem.at[i], recv_sem=r_sem.at[i],
                device_id={"space": p}, device_id_type=MESH,
            )
            c.start()
            out.append(c)
        return out

    def share(src, dst, s_sem, r_sem):
        out = []
        for o in range(1, beads):
            c = pltpu.make_async_remote_copy(
                src_ref=src, dst_ref=dst.at[o], send_sem=s_sem.at[o], recv_sem=r_sem.at[o],
                device_id={"bead": ring[o]}, device_id_type=MESH,
            )
            c.start()
            out.append(c)
        return out

    halo = to_near(
        (msg_up, msg_low, msg_up.at[16:24], msg_low.at[16:24]), (in_low, in_up, in_low2, in_up2), fs_sem, fr_sem
    )
    prepared = prepare(nbr, (emb, r1, r2, mix1, mix2, rd1, rd2), work)
    q_copies = share(q_src, q_all, qs_sem, qr_sem)
    for c in halo:
        c.wait()

    def whole(ref):
        return both(ref[0:8, :]) + both(ref[8:16, :])

    ext_own = both(in_low[16:24, :]) + own_t + both(in_up[16:24, :])
    ext_low = both(in_low2[...]) + whole(in_low) + ghosts[0]
    ext_up = ghosts[1] + whole(in_up) + both(in_up2[...])
    nb_t = [in_low[24:32, :].astype(I32), in_low[32:40, :].astype(I32)] + nbr_t
    nb_t = nb_t + [in_up[24:32, :].astype(I32), in_up[32:40, :].astype(I32)]
    energy_gradient(
        prepared, ext_own, ext_low, ext_up, nb_t, to_low, to_up, to_low2, to_up2, kept, *work,
    )
    copies = to_near(
        (to_up, to_low, to_up2, to_low2), (from_low, from_up, from_low2, from_up2), hs_sem, hr_sem
    )

    there = [spread(send[:, t * 128 : (t + 1) * 128] >> 7) for t in range(4)]
    iota8 = lax.broadcasted_iota(I32, (8, 128), 0)
    rhs = jnp.where(
        jnp.broadcast_to(send & 127, (128, 512)) == lax.broadcasted_iota(I32, (128, 512), 0), 1.0, 0.0
    ).astype(BF16)
    mass4 = HEAVY - (HEAVY - 1.0) * jnp.concatenate(
        [flags[:, t * 128 : (t + 1) * 128] for t in range(4)], 0
    )
    mass = jnp.concatenate([mass4, mass4, mass4], 0)
    p12 = rows12(mom)
    for c in copies:
        c.wait()

    his, los = [], []
    for c in range(3):
        parts = []
        for t in range(4):
            near_, far = (from_low, from_low2) if t < 2 else (from_up, from_up2)
            at, a12, a2 = 12 + c * 4 + t, 12 + c * 2 + t % 2, c * 2 + t % 2
            v = kept[at : at + 1, :] + near_[a12 : a12 + 1, :] + far[a2 : a2 + 1, :]
            parts.append(jnp.where(there[t] == iota8, spread(v), 0.0))
        m = jnp.concatenate(parts, 1)
        hi = m.astype(BF16).astype(F32)
        his.append(hi)
        los.append(m - hi)
    got = halves(dot_nt(jnp.concatenate(his + los, 0).astype(BF16), rhs))
    got = jnp.concatenate([got[c * 8 : c * 8 + 4] for c in range(3)], 0)
    kicked = p12 - (kept[0:12, :] + from_low[0:12, :] + from_up[0:12, :] + got)
    p_src[...] = kicked
    p_copies = share(p_src, p_all, ps_sem, pr_sem)

    turn, reach, stiff = ring_tables(beads)
    q = q_src[...]
    qa, qs = turn[0] * q, stiff[0] * q
    for o, c in zip(range(1, beads), q_copies):
        c.wait()
        q = q_all[o]
        qa, qs = qa + turn[o] * q, qs + stiff[o] * q
    pa, pr = turn[0] * kicked, reach[0] * kicked
    for o, c in zip(range(1, beads), p_copies):
        c.wait()
        p = p_all[o]
        pa, pr = pa + turn[o] * p, pr + reach[o] * p
    qn = qa + pr / mass
    pn = pa - mass * qs
    for c in range(3):
        for t in range(4):
            at = c * 4 + t
            new_pos[c, 0:1, t * 128 : (t + 1) * 128] = qn[at : at + 1]
            new_mom[c, 0:1, t * 128 : (t + 1) * 128] = pn[at : at + 1]


def shards(
    positions, momenta, species, neighbours, send_list, embedding,
    radial_one, radial_two, mix_one, mix_two, read_one, read_two,
):
    domains, beads = lax.axis_size("space"), lax.axis_size("bead")
    dma = lambda n: pltpu.SemaphoreType.DMA((n,))
    rows = lambda n: pltpu.VMEM((n, 128), F32)
    q, p = pl.pallas_call(
        lambda *refs: step_kernel(domains, beads, *refs),
        out_shape=(jax.ShapeDtypeStruct((3, 1, 512), F32),) * 2,
        in_specs=[VM] * 12,
        out_specs=(VM,) * 2,
        scratch_shapes=[rows(n) for n in (40, 40, 40, 40, 8, 8, 24, 24, 8, 8, 24, 24, 24, 8, 8, 12, 12)]
        + [pltpu.VMEM((beads, 12, 128), F32)] * 2
        + [dma(4)] * 4 + [dma(beads)] * 4 + COMPUTE_SCRATCH,
        compiler_params=pltpu.CompilerParams(
            collective_id=0, has_side_effects=True, vmem_limit_bytes=60 << 20
        ),
        name="md_step",
    )(
        jnp.transpose(positions, (1, 0, 2)), jnp.transpose(momenta, (1, 0, 2)), species[None], neighbours,
        send_list[None], embedding, radial_one, radial_two, mix_one, mix_two, read_one[None], read_two[None],
    )
    return jnp.transpose(q, (1, 0, 2)), jnp.transpose(p, (1, 0, 2))


def solution(mesh):
    beads = P("bead", None, "space")
    placed = (beads, beads, P("space"), P(None, "space"), P("space")) + (P(),) * 7
    return jax.shard_map(shards, mesh=mesh, in_specs=placed, out_specs=(beads, beads), check_vma=False)
```

```python
import math

import numpy as np

import jax
import jax.numpy as jnp
from jax import lax
from jax.experimental import pallas as pl
from jax.experimental.pallas import tpu as pltpu
from jax.sharding import PartitionSpec as P

STEP = 2.0
HEAVY = 16.0
SQRT3 = math.sqrt(3.0)
SQRT5 = math.sqrt(5.0)
SQRT15 = math.sqrt(15.0)
F32 = jnp.float32
BF16 = jnp.bfloat16
I32 = jnp.int32
NT = (((1,), (1,)), ((), ()))
VM = pl.BlockSpec(memory_space=pltpu.VMEM)
SM = pl.BlockSpec(memory_space=pltpu.SMEM)
MESH = pl.DeviceIdType.MESH


def dot(a, b):
    return jnp.dot(a, b, preferred_element_type=F32)


def dot_nt(a, b):
    return lax.dot_general(a, b, NT, preferred_element_type=F32)


def split(x):
    hi = x.astype(BF16)
    return hi, (x - hi.astype(F32)).astype(BF16)


def halves(x):
    n = x.shape[0] // 2
    return x[:n] + x[n:]


def lane_take(tiles, idx):
    low = idx & 127
    high = idx >> 7
    out = jnp.take_along_axis(tiles[0], low, axis=1)
    for t in range(1, len(tiles)):
        out = jnp.where(high == t, jnp.take_along_axis(tiles[t], low, axis=1), out)
    return out


def spread(row, count=8):
    return jnp.broadcast_to(row, (count, row.shape[1]))


def build_hot(nbr, hot):
    @pl.loop(0, 8)
    def _(rc):
        at = pl.multiple_of(rc * 128, 128)
        ids = lax.broadcasted_iota(I32, (128, 128), 0) + at
        for it in range(4):
            for k in range(8):
                row = jnp.broadcast_to(nbr[k : k + 1, it * 128 : (it + 1) * 128], (128, 128))
                hot[it * 8 + k, pl.ds(at, 128), :] = jnp.where(ids == row, 1.0, 0.0).astype(BF16)


def prepare(nbr, weights, work):
    emb, r1, r2, mix1, mix2, rd1, rd2 = weights
    hot, two, lam = work[4], work[14], work[18]
    build_hot(nbr, hot)
    two[...] = jnp.zeros_like(two)
    lane_ids = lax.broadcasted_iota(I32, (128, 512), 0)
    for k in range(8):
        row = jnp.broadcast_to(nbr[k : k + 1, :] & 127, (128, 512))
        one = jnp.where(row == lane_ids, 1.0, 0.0).astype(BF16)
        for t in range(4):
            lam[k * 4 + t] = one[:, t * 128 : (t + 1) * 128]
    w_rows = []
    for f in range(2):
        for n in range(8):
            w_rows.append(spread(r1[n : n + 1, :] * emb[f : f + 1, :] * 0.125))
    wt = jnp.concatenate(w_rows, axis=0)
    wth, wtl = split(wt)
    wh, wl = split(jnp.transpose(wt))
    zero = jnp.zeros((128, 128), BF16)
    wf = jnp.concatenate([jnp.concatenate([wh, wh], 1), jnp.concatenate([wl, zero], 1)], 0)
    wtf = jnp.concatenate([jnp.concatenate([wth, wth], 1), jnp.concatenate([wtl, zero], 1)], 0)
    r2s = r2[...] * 0.125
    rows = jnp.concatenate([emb[...], rd1[...], rd2[...], jnp.zeros((4, 128), F32), r2s], 0)
    colmat = jnp.transpose(jnp.concatenate([rows, jnp.zeros((112, 128), F32)], 0))
    e0, e1 = colmat[:, 0:1], colmat[:, 1:2]
    c_rd1, c_rd2 = colmat[:, 2:3], colmat[:, 3:4]
    m1h, m1l = split(mix1[...])
    m1s = jnp.concatenate([m1h, m1l], 0)
    m1t = jnp.transpose(mix1[...])
    m1th, m1tl = split(m1t)
    m1ts = jnp.concatenate([m1th, m1tl], 0)
    m2h, m2l = split(mix2[...])
    m2s = jnp.concatenate([m2h, m2l], 0)
    m2th, m2tl = split(jnp.transpose(mix2[...]))
    m2ts = jnp.concatenate([m2th, m2tl], 0)
    r2th, r2tl = split(colmat[:, 8:16])
    r2lhs = jnp.concatenate([r2th.astype(F32), r2th.astype(F32), r2tl.astype(F32)], 1).astype(BF16)
    r2h, r2l = split(r2s)
    r2f = jnp.concatenate(
        [jnp.concatenate([r2h, r2h], 1).astype(F32), jnp.concatenate([r2l, jnp.zeros_like(r2l)], 1).astype(F32)], 0
    ).astype(BF16)
    return wf, wtf, e0, e1, c_rd1, c_rd2, m1h, m1s, m1th, m1ts, m2h, m2s, m2th, m2ts, r2s, r2lhs, r2f


def energy_gradient(
    here, prepared, ext_own, nb_own, rest, send_early,
    to_low, to_up, to_low2, to_up2, to_low_s, to_up_s, kept,
    nb_s, geo, yy, bb, hot, m1, hs, ds1, gg, ww, m2, dg, dw, part, two, dh, dr, fl, lam, lam_g,
):
    (wf, wtf, e0, e1, c_rd1, c_rd2, m1h, m1s, m1th, m1ts, m2h, m2s, m2th, m2ts, r2s, r2lhs, r2f) = prepared
    def geometry(e, ext, idx):
        cols = slice(e * 128, (e + 1) * 128)
        nb_s[:, cols] = idx
        fl[:, cols] = spread(ext_own[e][3:4])
        got = [lane_take([spread(x[c : c + 1]) for x in ext], idx) for c in range(4)]
        rx, ry, rz = [got[c] - spread(ext_own[e][c : c + 1]) for c in range(3)]
        s = jnp.sqrt(rx * rx + ry * ry + rz * rz + 1.0)
        inv = 1.0 / s
        ux, uy, uz = rx * inv, ry * inv, rz * inv
        for c, v in enumerate((ux, uy, uz, s, inv, got[3])):
            geo[c, :, cols] = v
        ys = (
            SQRT3 * ux, SQRT3 * uy, SQRT3 * uz,
            SQRT15 * ux * uy, SQRT15 * uy * uz,
            0.5 * SQRT5 * (2.0 * uz * uz - ux * ux - uy * uy),
            SQRT15 * ux * uz, 0.5 * SQRT15 * (ux * ux - uy * uy),
        )
        for l in range(8):
            yy[l, :, cols] = ys[l]
        for n in range(8):
            bb[n, :, cols] = jnp.exp(-0.5 * (s - (1.0 + n)) ** 2)

    def mixed(ws, wh_, x):
        hi, lo = split(x)
        return halves(dot(ws, hi)) + dot(wh_, lo)

    def forward(ch):
        sl = slice(ch * 256, (ch + 1) * 256)
        f = geo[5, :, sl]
        bs = []
        for n in range(8):
            bs.append(bb[n, :, sl] * (1.0 - f))
        for n in range(8):
            bs.append(bb[n, :, sl] * f)
        q = [None, None, None]
        for l in range(9):
            z = jnp.concatenate(bs if l == 0 else [yy[l - 1, :, sl] * b for b in bs], 0)
            m = halves(dot(wf, jnp.concatenate(split(z), 0)))
            m1[l, :, sl] = m
            g = 0 if l == 0 else (1 if l < 4 else 2)
            q[g] = m * m if q[g] is None else q[g] + m * m
        v = mixed(m1s, m1h, jnp.concatenate(q, 0))
        sg = 1.0 / (1.0 + jnp.exp(-v))
        fc = fl[0:1, sl]
        h = e0 + fc * (e1 - e0) + v * sg
        ds1[:, sl] = sg * (1.0 + v * (1.0 - sg))
        hh = jnp.concatenate(split(h), 0)
        for o in range(2):
            hs[2 * ch + o] = hh[:, o * 128 : (o + 1) * 128]

    for e in range(2, 6):
        geometry(e, ext_own, nb_own[e - 2])

    @pl.when(here >= 0)
    def _():
        forward(1)
        forward(2)

    ext_low, ext_up, nb_ghost = rest()
    for o, e in enumerate((0, 1, 6, 7)):
        geometry(e, ext_low if e < 2 else ext_up, nb_ghost[o])

    @pl.when(here >= -1)
    def _():
        forward(0)
        forward(3)

    lane_ids = lax.broadcasted_iota(I32, (128, 128), 0)
    for k in range(8):
        for o, e in enumerate((0, 1, 6, 7)):
            row = jnp.broadcast_to(nb_s[k : k + 1, e * 128 : (e + 1) * 128] & 127, (128, 128))
            lam_g[k * 4 + o] = jnp.where(row == lane_ids, 1.0, 0.0).astype(BF16)

    own_lanes = slice(256, 768)
    iota8 = lax.broadcasted_iota(I32, (8, 256), 0).astype(F32)

    def own_at(it):
        return slice(256 + it * 128, 384 + it * 128)

    def basis(k, it):
        row = jnp.concatenate([geo[3, k : k + 1, own_at(it)], geo[3, k + 1 : k + 2, own_at(it)]], 1)
        off = spread(row) - 1.0 - iota8
        return off, jnp.exp(-0.5 * off * off)

    def gather(it, cc):
        at = it * 8 + 2 * cc
        feats = jnp.concatenate([hs[t] for t in range(8)], 1)
        got = halves(dot(feats, jnp.concatenate([hot[at], hot[at + 1]], 1)))
        _, bk = basis(2 * cc, it)
        bh, bl = split(bk)
        rhs = jnp.concatenate([bh.astype(F32), bl.astype(F32), bh.astype(F32)], 0).astype(BF16)
        wgt = dot(r2lhs, rhs)
        for o in range(2):
            gg[it, 2 * cc + o] = got[:, o * 128 : (o + 1) * 128]
            ww[it, 2 * cc + o] = wgt[:, o * 128 : (o + 1) * 128]

    def y_row(l, k, it):
        return yy[l - 1, k : k + 1, own_at(it)]

    def moments(it, cc):
        rows_ = slice(cc * 32, cc * 32 + 32)
        car = [gg[it, k, rows_] * ww[it, k, rows_] for k in range(8)]
        acc = car[0]
        for k in range(1, 8):
            acc = acc + car[k]
        m2[it, 0, rows_] = acc
        for l in range(1, 9):
            acc = y_row(l, 0, it) * car[0]
            for k in range(1, 8):
                acc = acc + y_row(l, k, it) * car[k]
            m2[it, l, rows_] = acc

    def middle(it):
        q = [None, None, None]
        for l in range(9):
            m = m2[it, l]
            g = 0 if l == 0 else (1 if l < 4 else 2)
            q[g] = m * m if q[g] is None else q[g] + m * m
        v = mixed(m2s, m2h, jnp.concatenate(q, 0))
        sg = 1.0 / (1.0 + jnp.exp(-v))
        dv = c_rd2 * (sg * (1.0 + v * (1.0 - sg)))
        dq = mixed(m2ts, m2th, dv) * 2.0
        for l in range(9):
            g = 0 if l == 0 else (1 if l < 4 else 2)
            m2[it, l] = m2[it, l] * dq[g * 128 : (g + 1) * 128]

    def backward(it, cc):
        rows_ = slice(cc * 32, cc * 32 + 32)
        rows_lo = slice(128 + cc * 32, 160 + cc * 32)
        lanes = slice(it * 128, (it + 1) * 128)
        dm = [m2[it, l, rows_] for l in range(9)]
        for k in range(8):
            g, w = gg[it, k, rows_], ww[it, k, rows_]
            car = g * w
            dcar = dm[0]
            for l in range(1, 9):
                dcar = dcar + y_row(l, k, it) * dm[l]
            for l in range(1, 9):
                pr = dm[l] * car
                pr = (pr[0:8] + pr[8:16]) + (pr[16:24] + pr[24:32])
                at8 = ((l - 1) * 8 + k) * 8
                part[at8 : at8 + 8, lanes] = pr if cc == 0 else part[at8 : at8 + 8, lanes] + pr
            hi, lo = split(dcar * w)
            dg[it * 8 + k, rows_] = hi
            dg[it * 8 + k, rows_lo] = lo
            hi, lo = split(dcar * g)
            dw[it * 8 + k, rows_] = hi
            dw[it * 8 + k, rows_lo] = lo

    def scatter(it, cc):
        cols = slice(cc * 256, (cc + 1) * 256)
        cot = jnp.concatenate([dg[it * 8 + k] for k in range(8)], 1)
        res = halves(dot_nt(cot, jnp.concatenate([hot[it * 8 + k, cols] for k in range(8)], 1)))
        dh[:, cols] = res if it == 0 else dh[:, cols] + res

    for cc in range(4):
        gather(0, cc)
    for it in range(4):
        for cc in range(4):
            if it < 3:
                gather(it + 1, cc)
            moments(it, cc)
    for it in range(4):
        middle(it)
    for it in range(4):
        for cc in range(4):
            if it:
                scatter(it - 1, cc)
            backward(it, cc)
    for cc in range(4):
        scatter(3, cc)
    for it in range(4):
        for cc in range(4):
            at = it * 8 + 2 * cc
            dbk = halves(dot(r2f, jnp.concatenate([dw[at], dw[at + 1]], 1)))
            off, bk = basis(2 * cc, it)
            res = -(dbk * bk * off)
            for o in range(2):
                at = 512 + (2 * cc + o) * 8
                part[at : at + 8, it * 128 : (it + 1) * 128] = res[:, o * 128 : (o + 1) * 128]
    sel = (lax.broadcasted_iota(I32, (72, 576), 1) >> 3) == lax.broadcasted_iota(I32, (72, 576), 0)
    sel = jnp.where(sel, 1.0, 0.0).astype(BF16)
    ph, pl_ = split(part[...])
    two[:, own_lanes] = dot(sel, ph) + dot(sel, pl_)

    def backward_one(ch):
        sl = slice(ch * 256, (ch + 1) * 256)
        dv = (dh[:, sl] + c_rd1 if ch in (1, 2) else dh[:, sl]) * ds1[:, sl]
        dq = mixed(m1ts, m1th, dv) * 2.0
        on = geo[5, :, sl] > 0.5
        ux, uy, uz = geo[0, :, sl], geo[1, :, sl], geo[2, :, sl]
        s, inv = geo[3, :, sl], geo[4, :, sl]
        bs = [bb[n, :, sl] for n in range(8)]
        dy, db = [None], [None] * 8
        for l in range(9):
            g = 0 if l == 0 else (1 if l < 4 else 2)
            dm = m1[l, :, sl] * dq[g * 128 : (g + 1) * 128]
            dz = halves(dot(wtf, jnp.concatenate(split(dm), 0)))
            y = None if l == 0 else yy[l - 1, :, sl]
            acc = None
            for n in range(8):
                t = jnp.where(on, dz[64 + n * 8 : 72 + n * 8], dz[n * 8 : n * 8 + 8])
                if l == 0:
                    db[n] = t
                else:
                    db[n] = db[n] + t * y
                    acc = t * bs[n] if acc is None else acc + t * bs[n]
            if l:
                dy.append(acc + two[(l - 1) * 8 : l * 8, sl])
        dsv = two[64:72, sl]
        for n in range(8):
            dsv = dsv - db[n] * bs[n] * (s - (1.0 + n))
        dux = SQRT3 * dy[1] + SQRT15 * (uy * dy[4] + uz * dy[7] + ux * dy[8]) - SQRT5 * ux * dy[6]
        duy = SQRT3 * dy[2] + SQRT15 * (ux * dy[4] + uz * dy[5] - uy * dy[8]) - SQRT5 * uy * dy[6]
        duz = SQRT3 * dy[3] + SQRT15 * (uy * dy[5] + ux * dy[7]) + 2.0 * SQRT5 * uz * dy[6]
        along = dsv - (dux * ux + duy * uy + duz * uz) * inv
        dr[0, :, sl] = dux * inv + ux * along
        dr[1, :, sl] = duy * inv + uy * along
        dr[2, :, sl] = duz * inv + uz * along

    def onto(first, count, hots):
        tile_ids = lax.broadcasted_iota(I32, (8, count), 0)
        acc = jnp.zeros((48, 128), F32)
        for k in range(8):
            there = spread(nb_s[k : k + 1, first : first + count] >> 7) == tile_ids
            his, los = [], []
            for c in range(3):
                m = jnp.where(there, spread(dr[c, k : k + 1, first : first + count]), 0.0)
                hi = m.astype(BF16).astype(F32)
                his.append(hi)
                los.append(m - hi)
            lhs = jnp.concatenate(his + los, 0).astype(BF16)
            acc = acc + dot_nt(lhs, jnp.concatenate(hots(k), 1))
        return halves(acc)

    def put(ref, at, acc, c, first, count):
        ref[at : at + count, :] = acc[c * 8 + first : c * 8 + first + count, :]

    for ref in (to_low2, to_up2, to_low_s, to_up_s):
        ref[6:8, :] = jnp.zeros((2, 128), F32)
    for ref in (to_low, to_up):
        ref[12:16, :] = jnp.zeros((4, 128), F32)

    @pl.when(here >= 0)
    def _():
        backward_one(0)
        backward_one(3)

    acc_low = onto(0, 256, lambda k: [lam_g[k * 4], lam_g[k * 4 + 1]])
    acc_up = onto(768, 256, lambda k: [lam_g[k * 4 + 2], lam_g[k * 4 + 3]])
    for c in range(3):
        put(kept, 12 + c * 4, acc_low, c, 6, 2)
        put(kept, 14 + c * 4, acc_up, c, 0, 2)
        put(to_low, c * 4, acc_low, c, 2, 4)
        put(to_up, c * 4, acc_up, c, 2, 4)
        put(to_low2, c * 2, acc_low, c, 0, 2)
        put(to_up2, c * 2, acc_up, c, 6, 2)
    send_early()

    @pl.when(here >= -1)
    def _():
        backward_one(1)
        backward_one(2)

    selfs = [jnp.sum(dr[c], axis=0, keepdims=True) for c in range(3)]
    selfs = jnp.concatenate([v[:, t * 128 : (t + 1) * 128] for v in selfs for t in range(8)], 0)
    acc_own = onto(256, 512, lambda k: [lam[k * 4 + t] for t in range(4)]) - selfs
    for c in range(3):
        put(kept, c * 4, acc_own, c, 2, 4)
        put(to_low_s, c * 2, acc_own, c, 0, 2)
        put(to_up_s, c * 2, acc_own, c, 6, 2)


COMPUTE_SCRATCH = [
    pltpu.VMEM((8, 1024), I32),
    pltpu.VMEM((6, 8, 1024), F32),
    pltpu.VMEM((8, 8, 1024), F32),
    pltpu.VMEM((8, 8, 1024), F32),
    pltpu.VMEM((32, 1024, 128), BF16),
    pltpu.VMEM((9, 128, 1024), F32),
    pltpu.VMEM((8, 256, 128), BF16),
    pltpu.VMEM((128, 1024), F32),
    pltpu.VMEM((4, 8, 128, 128), F32),
    pltpu.VMEM((4, 8, 128, 128), F32),
    pltpu.VMEM((4, 9, 128, 128), F32),
    pltpu.VMEM((32, 256, 128), BF16),
    pltpu.VMEM((32, 256, 128), BF16),
    pltpu.VMEM((576, 512), F32),
    pltpu.VMEM((72, 1024), F32),
    pltpu.VMEM((128, 1024), F32),
    pltpu.VMEM((3, 8, 1024), F32),
    pltpu.VMEM((8, 1024), F32),
    pltpu.VMEM((32, 128, 128), BF16),
    pltpu.VMEM((32, 128, 128), BF16),
]


def ring_tables(beads):
    b = np.arange(beads, dtype=np.float64)
    angle = beads * np.sin(np.pi * b / beads)
    safe = np.where(b == 0, 1.0, angle)
    reach = np.where(b == 0, STEP, STEP * np.sin(angle) / safe)
    stiff = angle * np.sin(angle) / STEP
    phase = np.cos(2.0 * np.pi * np.outer(b, b) / beads) / beads
    return [(phase @ f).tolist() for f in (np.cos(angle), reach, stiff)]


def rows12(ref):
    return jnp.concatenate([ref[c, 0:1, t * 128 : (t + 1) * 128] for c in range(3) for t in range(4)], 0)


def step_kernel(
    domains, beads,
    pos, mom, spec, nbr, send_ref, emb, r1, r2, mix1, mix2, rd1, rd2,
    packed,
    msg_up, msg_low, in_low, in_up, in_low2, in_up2,
    to_low, to_up, to_low2, to_up2, to_low_s, to_up_s, kept,
    from_low, from_up, from_low2, from_up2, from_low_s, from_up_s, q_src, p_src, q_all, p_all,
    fs_sem, fr_sem, hs_sem, hr_sem, qs_sem, qr_sem, ps_sem, pr_sem,
    *work,
):
    me = lax.axis_index("space")
    bead = lax.axis_index("bead")
    near = [lax.rem(me + s + domains, domains) for s in (1, -1, 2, -2)]
    ring = [lax.rem(bead + o, beads) for o in range(beads)]
    barrier = pltpu.get_barrier_semaphore()
    for p in near:
        pl.semaphore_signal(barrier, inc=1, device_id={"space": p}, device_id_type=MESH)
    for o in range(1, beads):
        pl.semaphore_signal(barrier, inc=1, device_id={"bead": ring[o]}, device_id_type=MESH)

    flags = spec[...].astype(F32)
    send = send_ref[...]
    own_t, nbr_t = [], []
    for t in range(4):
        lanes = slice(t * 128, (t + 1) * 128)
        quad = [pos[c, 0:1, lanes] for c in range(3)] + [flags[:, lanes]]
        own_t.append(jnp.concatenate(quad + quad, 0))
        nbr_t.append(nbr[:, lanes])

    def sent(tiles, half):
        return [
            lane_take(tiles, spread(send[:, at : at + 128])) for at in (half * 256, half * 256 + 128)
        ]

    def pair(x, y):
        return jnp.concatenate([x[0:4], y[4:8]], 0)

    def both(x):
        return [jnp.concatenate([x[0:4], x[0:4]], 0), jnp.concatenate([x[4:8], x[4:8]], 0)]

    ghosts = [sent(own_t, 0), sent(own_t, 1)]
    q_src[...] = rows12(pos)
    for msg, half in ((msg_low, 0), (msg_up, 1)):
        lists = sent(nbr_t, half)
        msg[0:8, :] = pair(*ghosts[half])
        msg[8:16, :] = pair(own_t[0], own_t[1])
        msg[16:24, :] = pair(own_t[2], own_t[3])
        msg[24:32, :] = lists[0].astype(F32)
        msg[32:40, :] = lists[1].astype(F32)
    pl.semaphore_wait(barrier, 4 + beads - 1)

    def to_near(first, peers, srcs, dsts, s_sem, r_sem):
        out = []
        for i, p, s, dst in zip(range(first, 6), peers, srcs, dsts):
            c = pltpu.make_async_remote_copy(
                src_ref=s, dst_ref=dst, send_sem=s_sem.at[i], recv_sem=r_sem.at[i],
                device_id={"space": p}, device_id_type=MESH,
            )
            c.start()
            out.append(c)
        return out

    def share(src, dst, s_sem, r_sem):
        out = []
        for o in range(1, beads):
            c = pltpu.make_async_remote_copy(
                src_ref=src, dst_ref=dst.at[o], send_sem=s_sem.at[o], recv_sem=r_sem.at[o],
                device_id={"bead": ring[o]}, device_id_type=MESH,
            )
            c.start()
            out.append(c)
        return out

    edge = (msg_up.at[0:8], msg_low.at[0:8])
    halo = to_near(0, near, edge, (in_low.at[0:8], in_up.at[0:8]), fs_sem, fr_sem)
    bulk = to_near(
        2, near, (msg_up.at[8:40], msg_low.at[8:40]) + edge, (in_low.at[8:40], in_up.at[8:40], in_low2, in_up2),
        fs_sem, fr_sem,
    )
    prepared = prepare(nbr, (emb, r1, r2, mix1, mix2, rd1, rd2), work)
    q_copies = share(q_src, q_all, qs_sem, qr_sem)
    for c in halo:
        c.wait()

    def whole(ref):
        return both(ref[8:16, :]) + both(ref[16:24, :])

    def rest():
        for c in bulk:
            c.wait()
        ext_low = both(in_low2[...]) + whole(in_low) + ghosts[0]
        ext_up = ghosts[1] + whole(in_up) + both(in_up2[...])
        return ext_low, ext_up, [r[a : a + 8, :].astype(I32) for r in (in_low, in_up) for a in (24, 32)]

    copies = []

    def send_early():
        copies.extend(
            to_near(0, near, (to_up, to_low, to_up2, to_low2), (from_low, from_up, from_low2, from_up2), hs_sem, hr_sem)
        )

    ext_own = both(in_low[0:8, :]) + own_t + both(in_up[0:8, :])
    energy_gradient(
        me, prepared, ext_own, nbr_t, rest, send_early,
        to_low, to_up, to_low2, to_up2, to_low_s, to_up_s, kept, *work,
    )
    copies += to_near(4, near, (to_up_s, to_low_s), (from_low_s, from_up_s), hs_sem, hr_sem)

    there = [spread(send[:, t * 128 : (t + 1) * 128] >> 7) for t in range(4)]
    iota8 = lax.broadcasted_iota(I32, (8, 128), 0)
    rhs = jnp.where(
        jnp.broadcast_to(send & 127, (128, 512)) == lax.broadcasted_iota(I32, (128, 512), 0), 1.0, 0.0
    ).astype(BF16)
    mass4 = HEAVY - (HEAVY - 1.0) * jnp.concatenate(
        [flags[:, t * 128 : (t + 1) * 128] for t in range(4)], 0
    )
    mass = jnp.concatenate([mass4, mass4, mass4], 0)
    p12 = rows12(mom)
    for c in copies:
        c.wait()

    his, los = [], []
    for c in range(3):
        parts = []
        for t in range(4):
            near_, far = (from_low_s, from_low2) if t < 2 else (from_up_s, from_up2)
            at, a2 = 12 + c * 4 + t, c * 2 + t % 2
            v = kept[at : at + 1, :] + near_[a2 : a2 + 1, :] + far[a2 : a2 + 1, :]
            parts.append(jnp.where(there[t] == iota8, spread(v), 0.0))
        m = jnp.concatenate(parts, 1)
        hi = m.astype(BF16).astype(F32)
        his.append(hi)
        los.append(m - hi)
    got = halves(dot_nt(jnp.concatenate(his + los, 0).astype(BF16), rhs))
    got = jnp.concatenate([got[c * 8 : c * 8 + 4] for c in range(3)], 0)
    kicked = p12 - (kept[0:12, :] + from_low[0:12, :] + from_up[0:12, :] + got)
    p_src[...] = kicked
    p_copies = share(p_src, p_all, ps_sem, pr_sem)

    turn, reach, stiff = ring_tables(beads)
    q = q_src[...]
    qa, qs = turn[0] * q, stiff[0] * q
    for o, c in zip(range(1, beads), q_copies):
        c.wait()
        q = q_all[o]
        qa, qs = qa + turn[o] * q, qs + stiff[o] * q
    pa, pr = turn[0] * kicked, reach[0] * kicked
    for o, c in zip(range(1, beads), p_copies):
        c.wait()
        p = p_all[o]
        pa, pr = pa + turn[o] * p, pr + reach[o] * p
    for i, v in enumerate((qa, pr / mass, pa, mass * qs)):
        for c in range(3):
            for t in range(4):
                at = c * 4 + t
                packed[i, c, 0:1, t * 128 : (t + 1) * 128] = v[at : at + 1]


def shards(
    positions, momenta, species, neighbours, send_list, embedding,
    radial_one, radial_two, mix_one, mix_two, read_one, read_two,
):
    domains, beads = lax.axis_size("space"), lax.axis_size("bead")
    dma = lambda n: pltpu.SemaphoreType.DMA((n,))
    rows = lambda n: pltpu.VMEM((n, 128), F32)
    out = pl.pallas_call(
        lambda *refs: step_kernel(domains, beads, *refs),
        out_shape=jax.ShapeDtypeStruct((4, 3, 1, 512), F32),
        in_specs=[VM] * 12,
        out_specs=VM,
        scratch_shapes=[rows(n) for n in (40, 40, 40, 40, 8, 8, 16, 16, 8, 8, 8, 8, 24, 16, 16, 8, 8, 8, 8, 12, 12)]
        + [pltpu.VMEM((beads, 12, 128), F32)] * 2
        + [dma(6)] * 4 + [dma(beads)] * 4 + COMPUTE_SCRATCH,
        compiler_params=pltpu.CompilerParams(
            collective_id=0, has_side_effects=True, vmem_limit_bytes=60 << 20
        ),
        name="md_step",
    )(
        jnp.transpose(positions, (1, 0, 2)), jnp.transpose(momenta, (1, 0, 2)), species[None], neighbours,
        send_list[None], embedding, radial_one, radial_two, mix_one, mix_two, read_one[None], read_two[None],
    )
    return jnp.transpose(out[0] + out[1], (1, 0, 2)), jnp.transpose(out[2] - out[3], (1, 0, 2))


def solution(mesh):
    beads = P("bead", None, "space")
    placed = (beads, beads, P("space"), P(None, "space"), P("space")) + (P(),) * 7
    return jax.shard_map(shards, mesh=mesh, in_specs=placed, out_specs=(beads, beads), check_vma=False)
```

```python
import math

import numpy as np

import jax
import jax.numpy as jnp
from jax import lax
from jax.experimental import pallas as pl
from jax.experimental.pallas import tpu as pltpu
from jax.sharding import PartitionSpec as P

STEP = 2.0
HEAVY = 16.0
SQRT3 = math.sqrt(3.0)
SQRT5 = math.sqrt(5.0)
SQRT15 = math.sqrt(15.0)
F32 = jnp.float32
BF16 = jnp.bfloat16
I32 = jnp.int32
NT = (((1,), (1,)), ((), ()))
VM = pl.BlockSpec(memory_space=pltpu.VMEM)
SM = pl.BlockSpec(memory_space=pltpu.SMEM)
MESH = pl.DeviceIdType.MESH


def dot(a, b):
    return jnp.dot(a, b, preferred_element_type=F32)


def dot_nt(a, b):
    return lax.dot_general(a, b, NT, preferred_element_type=F32)


def split(x):
    hi = x.astype(BF16)
    return hi, (x - hi.astype(F32)).astype(BF16)


def halves(x):
    n = x.shape[0] // 2
    return x[:n] + x[n:]


def lane_take(tiles, idx):
    low = idx & 127
    high = idx >> 7
    out = jnp.take_along_axis(tiles[0], low, axis=1)
    for t in range(1, len(tiles)):
        out = jnp.where(high == t, jnp.take_along_axis(tiles[t], low, axis=1), out)
    return out


def spread(row, count=8):
    return jnp.broadcast_to(row, (count, row.shape[1]))


def build_hot(nbr, hot):
    @pl.loop(0, 8)
    def _(rc):
        at = pl.multiple_of(rc * 128, 128)
        ids = lax.broadcasted_iota(I32, (128, 128), 0) + at
        for it in range(4):
            for k in range(8):
                row = jnp.broadcast_to(nbr[k : k + 1, it * 128 : (it + 1) * 128], (128, 128))
                hot[it * 8 + k, pl.ds(at, 128), :] = jnp.where(ids == row, 1.0, 0.0).astype(BF16)


def prepare(nbr, weights, work):
    emb, r1, r2, mix1, mix2, rd1, rd2 = weights
    hot, two, lam = work[4], work[14], work[18]
    build_hot(nbr, hot)
    two[...] = jnp.zeros_like(two)
    lane_ids = lax.broadcasted_iota(I32, (128, 512), 0)
    for k in range(8):
        row = jnp.broadcast_to(nbr[k : k + 1, :] & 127, (128, 512))
        one = jnp.where(row == lane_ids, 1.0, 0.0).astype(BF16)
        for t in range(4):
            lam[k * 4 + t] = one[:, t * 128 : (t + 1) * 128]
    w_rows = []
    for f in range(2):
        for n in range(8):
            w_rows.append(spread(r1[n : n + 1, :] * emb[f : f + 1, :] * 0.125))
    wt = jnp.concatenate(w_rows, axis=0)
    wth, wtl = split(wt)
    wh, wl = split(jnp.transpose(wt))
    zero = jnp.zeros((128, 128), BF16)
    wf = jnp.concatenate([jnp.concatenate([wh, wh], 1), jnp.concatenate([wl, zero], 1)], 0)
    wtf = jnp.concatenate([jnp.concatenate([wth, wth], 1), jnp.concatenate([wtl, zero], 1)], 0)
    r2s = r2[...] * 0.125
    rows = jnp.concatenate([emb[...], rd1[...], rd2[...], jnp.zeros((4, 128), F32), r2s], 0)
    colmat = jnp.transpose(jnp.concatenate([rows, jnp.zeros((112, 128), F32)], 0))
    e0, e1 = colmat[:, 0:1], colmat[:, 1:2]
    c_rd1, c_rd2 = colmat[:, 2:3], colmat[:, 3:4]
    m1h, m1l = split(mix1[...])
    m1s = jnp.concatenate([m1h, m1l], 0)
    m1t = jnp.transpose(mix1[...])
    m1th, m1tl = split(m1t)
    m1ts = jnp.concatenate([m1th, m1tl], 0)
    m2h, m2l = split(mix2[...])
    m2s = jnp.concatenate([m2h, m2l], 0)
    m2th, m2tl = split(jnp.transpose(mix2[...]))
    m2ts = jnp.concatenate([m2th, m2tl], 0)
    r2th, r2tl = split(colmat[:, 8:16])
    r2lhs = jnp.concatenate([r2th.astype(F32), r2th.astype(F32), r2tl.astype(F32)], 1).astype(BF16)
    r2h, r2l = split(r2s)
    r2f = jnp.concatenate(
        [jnp.concatenate([r2h, r2h], 1).astype(F32), jnp.concatenate([r2l, jnp.zeros_like(r2l)], 1).astype(F32)], 0
    ).astype(BF16)
    return wf, wtf, e0, e1, c_rd1, c_rd2, m1h, m1s, m1th, m1ts, m2h, m2s, m2th, m2ts, r2s, r2lhs, r2f


def energy_gradient(
    here, prepared, ext_own, nb_own, rest, send_early,
    to_low, to_up, to_low2, to_up2, to_low_s, to_up_s, kept,
    nb_s, geo, yy, bb, hot, m1, hs, ds1, gg, ww, m2, dg, dw, part, two, dh, dr, fl, lam, lam_g,
):
    (wf, wtf, e0, e1, c_rd1, c_rd2, m1h, m1s, m1th, m1ts, m2h, m2s, m2th, m2ts, r2s, r2lhs, r2f) = prepared
    def geometry(e, ext, idx):
        cols = slice(e * 128, (e + 1) * 128)
        nb_s[:, cols] = idx
        fl[:, cols] = spread(ext_own[e][3:4])
        got = [lane_take([spread(x[c : c + 1]) for x in ext], idx) for c in range(4)]
        rx, ry, rz = [got[c] - spread(ext_own[e][c : c + 1]) for c in range(3)]
        s = jnp.sqrt(rx * rx + ry * ry + rz * rz + 1.0)
        inv = 1.0 / s
        ux, uy, uz = rx * inv, ry * inv, rz * inv
        for c, v in enumerate((ux, uy, uz, s, inv, got[3])):
            geo[c, :, cols] = v
        ys = (
            SQRT3 * ux, SQRT3 * uy, SQRT3 * uz,
            SQRT15 * ux * uy, SQRT15 * uy * uz,
            0.5 * SQRT5 * (2.0 * uz * uz - ux * ux - uy * uy),
            SQRT15 * ux * uz, 0.5 * SQRT15 * (ux * ux - uy * uy),
        )
        for l in range(8):
            yy[l, :, cols] = ys[l]
        for n in range(8):
            bb[n, :, cols] = jnp.exp(-0.5 * (s - (1.0 + n)) ** 2)

    def mixed(ws, wh_, x):
        hi, lo = split(x)
        return halves(dot(ws, hi)) + dot(wh_, lo)

    def forward(ch):
        sl = slice(ch * 256, (ch + 1) * 256)
        f = geo[5, :, sl]
        bs = []
        for n in range(8):
            bs.append(bb[n, :, sl] * (1.0 - f))
        for n in range(8):
            bs.append(bb[n, :, sl] * f)
        q = [None, None, None]
        for l in range(9):
            z = jnp.concatenate(bs if l == 0 else [yy[l - 1, :, sl] * b for b in bs], 0)
            m = halves(dot(wf, jnp.concatenate(split(z), 0)))
            m1[l, :, sl] = m
            g = 0 if l == 0 else (1 if l < 4 else 2)
            q[g] = m * m if q[g] is None else q[g] + m * m
        v = mixed(m1s, m1h, jnp.concatenate(q, 0))
        sg = 1.0 / (1.0 + jnp.exp(-v))
        fc = fl[0:1, sl]
        h = e0 + fc * (e1 - e0) + v * sg
        ds1[:, sl] = sg * (1.0 + v * (1.0 - sg))
        hh = jnp.concatenate(split(h), 0)
        for o in range(2):
            hs[2 * ch + o] = hh[:, o * 128 : (o + 1) * 128]

    for e in range(2, 6):
        geometry(e, ext_own, nb_own[e - 2])

    @pl.when(here >= 0)
    def _():
        forward(1)
        forward(2)

    ext_low, ext_up, nb_ghost = rest()
    for o, e in enumerate((0, 1, 6, 7)):
        geometry(e, ext_low if e < 2 else ext_up, nb_ghost[o])

    @pl.when(here >= -1)
    def _():
        forward(0)
        forward(3)

    lane_ids = lax.broadcasted_iota(I32, (128, 128), 0)
    for k in range(8):
        for o, e in enumerate((0, 1, 6, 7)):
            row = jnp.broadcast_to(nb_s[k : k + 1, e * 128 : (e + 1) * 128] & 127, (128, 128))
            lam_g[k * 4 + o] = jnp.where(row == lane_ids, 1.0, 0.0).astype(BF16)

    own_lanes = slice(256, 768)
    iota8 = lax.broadcasted_iota(I32, (8, 256), 0).astype(F32)

    def own_at(it):
        return slice(256 + it * 128, 384 + it * 128)

    def basis(k, it):
        row = jnp.concatenate([geo[3, k : k + 1, own_at(it)], geo[3, k + 1 : k + 2, own_at(it)]], 1)
        off = spread(row) - 1.0 - iota8
        return off, jnp.exp(-0.5 * off * off)

    def gather(it, cc):
        at = it * 8 + 2 * cc
        feats = jnp.concatenate([hs[t] for t in range(8)], 1)
        got = halves(dot(feats, jnp.concatenate([hot[at], hot[at + 1]], 1)))
        _, bk = basis(2 * cc, it)
        bh, bl = split(bk)
        rhs = jnp.concatenate([bh.astype(F32), bl.astype(F32), bh.astype(F32)], 0).astype(BF16)
        wgt = dot(r2lhs, rhs)
        for o in range(2):
            gg[it, 2 * cc + o] = got[:, o * 128 : (o + 1) * 128]
            ww[it, 2 * cc + o] = wgt[:, o * 128 : (o + 1) * 128]

    def y_row(l, k, it):
        return yy[l - 1, k : k + 1, own_at(it)]

    def moments(it, cc):
        rows_ = slice(cc * 32, cc * 32 + 32)
        car = [gg[it, k, rows_] * ww[it, k, rows_] for k in range(8)]
        acc = car[0]
        for k in range(1, 8):
            acc = acc + car[k]
        m2[it, 0, rows_] = acc
        for l in range(1, 9):
            acc = y_row(l, 0, it) * car[0]
            for k in range(1, 8):
                acc = acc + y_row(l, k, it) * car[k]
            m2[it, l, rows_] = acc

    def middle(it):
        q = [None, None, None]
        for l in range(9):
            m = m2[it, l]
            g = 0 if l == 0 else (1 if l < 4 else 2)
            q[g] = m * m if q[g] is None else q[g] + m * m
        v = mixed(m2s, m2h, jnp.concatenate(q, 0))
        sg = 1.0 / (1.0 + jnp.exp(-v))
        dv = c_rd2 * (sg * (1.0 + v * (1.0 - sg)))
        dq = mixed(m2ts, m2th, dv) * 2.0
        for l in range(9):
            g = 0 if l == 0 else (1 if l < 4 else 2)
            m2[it, l] = m2[it, l] * dq[g * 128 : (g + 1) * 128]

    def backward(it, cc):
        rows_ = slice(cc * 32, cc * 32 + 32)
        rows_lo = slice(128 + cc * 32, 160 + cc * 32)
        lanes = slice(it * 128, (it + 1) * 128)
        dm = [m2[it, l, rows_] for l in range(9)]
        for k in range(8):
            g, w = gg[it, k, rows_], ww[it, k, rows_]
            car = g * w
            dcar = dm[0]
            for l in range(1, 9):
                dcar = dcar + y_row(l, k, it) * dm[l]
            for l in range(1, 9):
                pr = dm[l] * car
                pr = (pr[0:8] + pr[8:16]) + (pr[16:24] + pr[24:32])
                at8 = ((l - 1) * 8 + k) * 8
                part[at8 : at8 + 8, lanes] = pr if cc == 0 else part[at8 : at8 + 8, lanes] + pr
            hi, lo = split(dcar * w)
            dg[it * 8 + k, rows_] = hi
            dg[it * 8 + k, rows_lo] = lo
            hi, lo = split(dcar * g)
            dw[it * 8 + k, rows_] = hi
            dw[it * 8 + k, rows_lo] = lo

    def scatter(it, cc):
        cols = slice(cc * 256, (cc + 1) * 256)
        cot = jnp.concatenate([dg[it * 8 + k] for k in range(8)], 1)
        res = halves(dot_nt(cot, jnp.concatenate([hot[it * 8 + k, cols] for k in range(8)], 1)))
        dh[:, cols] = res if it == 0 else dh[:, cols] + res

    for cc in range(4):
        gather(0, cc)
    for it in range(4):
        for cc in range(4):
            if it < 3:
                gather(it + 1, cc)
            moments(it, cc)
    for it in range(4):
        middle(it)
    for it in range(4):
        for cc in range(4):
            if it:
                scatter(it - 1, cc)
            backward(it, cc)
    for cc in range(4):
        scatter(3, cc)
    for it in range(4):
        for cc in range(4):
            at = it * 8 + 2 * cc
            dbk = halves(dot(r2f, jnp.concatenate([dw[at], dw[at + 1]], 1)))
            off, bk = basis(2 * cc, it)
            res = -(dbk * bk * off)
            for o in range(2):
                at = 512 + (2 * cc + o) * 8
                part[at : at + 8, it * 128 : (it + 1) * 128] = res[:, o * 128 : (o + 1) * 128]
    sel = (lax.broadcasted_iota(I32, (72, 576), 1) >> 3) == lax.broadcasted_iota(I32, (72, 576), 0)
    sel = jnp.where(sel, 1.0, 0.0).astype(BF16)
    ph, pl_ = split(part[...])
    two[:, own_lanes] = dot(sel, ph) + dot(sel, pl_)

    def backward_one(ch):
        sl = slice(ch * 256, (ch + 1) * 256)
        dv = (dh[:, sl] + c_rd1 if ch in (1, 2) else dh[:, sl]) * ds1[:, sl]
        dq = mixed(m1ts, m1th, dv) * 2.0
        on = geo[5, :, sl] > 0.5
        ux, uy, uz = geo[0, :, sl], geo[1, :, sl], geo[2, :, sl]
        s, inv = geo[3, :, sl], geo[4, :, sl]
        bs = [bb[n, :, sl] for n in range(8)]
        dy, db = [None], [None] * 8
        for l in range(9):
            g = 0 if l == 0 else (1 if l < 4 else 2)
            dm = m1[l, :, sl] * dq[g * 128 : (g + 1) * 128]
            dz = halves(dot(wtf, jnp.concatenate(split(dm), 0)))
            y = None if l == 0 else yy[l - 1, :, sl]
            acc = None
            for n in range(8):
                t = jnp.where(on, dz[64 + n * 8 : 72 + n * 8], dz[n * 8 : n * 8 + 8])
                if l == 0:
                    db[n] = t
                else:
                    db[n] = db[n] + t * y
                    acc = t * bs[n] if acc is None else acc + t * bs[n]
            if l:
                dy.append(acc + two[(l - 1) * 8 : l * 8, sl])
        dsv = two[64:72, sl]
        for n in range(8):
            dsv = dsv - db[n] * bs[n] * (s - (1.0 + n))
        dux = SQRT3 * dy[1] + SQRT15 * (uy * dy[4] + uz * dy[7] + ux * dy[8]) - SQRT5 * ux * dy[6]
        duy = SQRT3 * dy[2] + SQRT15 * (ux * dy[4] + uz * dy[5] - uy * dy[8]) - SQRT5 * uy * dy[6]
        duz = SQRT3 * dy[3] + SQRT15 * (uy * dy[5] + ux * dy[7]) + 2.0 * SQRT5 * uz * dy[6]
        along = dsv - (dux * ux + duy * uy + duz * uz) * inv
        dr[0, :, sl] = dux * inv + ux * along
        dr[1, :, sl] = duy * inv + uy * along
        dr[2, :, sl] = duz * inv + uz * along

    def onto(first, count, hots):
        tile_ids = lax.broadcasted_iota(I32, (8, count), 0)
        acc = jnp.zeros((48, 128), F32)
        for k in range(8):
            there = spread(nb_s[k : k + 1, first : first + count] >> 7) == tile_ids
            his, los = [], []
            for c in range(3):
                m = jnp.where(there, spread(dr[c, k : k + 1, first : first + count]), 0.0)
                hi = m.astype(BF16).astype(F32)
                his.append(hi)
                los.append(m - hi)
            lhs = jnp.concatenate(his + los, 0).astype(BF16)
            acc = acc + dot_nt(lhs, jnp.concatenate(hots(k), 1))
        return halves(acc)

    def put(ref, at, acc, c, first, count):
        ref[at : at + count, :] = acc[c * 8 + first : c * 8 + first + count, :]

    for ref in (to_low2, to_up2, to_low_s, to_up_s):
        ref[6:8, :] = jnp.zeros((2, 128), F32)
    for ref in (to_low, to_up):
        ref[12:16, :] = jnp.zeros((4, 128), F32)

    @pl.when(here >= 0)
    def _():
        backward_one(0)
        backward_one(3)

    acc_low = onto(0, 256, lambda k: [lam_g[k * 4], lam_g[k * 4 + 1]])
    acc_up = onto(768, 256, lambda k: [lam_g[k * 4 + 2], lam_g[k * 4 + 3]])
    for c in range(3):
        put(kept, 12 + c * 4, acc_low, c, 6, 2)
        put(kept, 14 + c * 4, acc_up, c, 0, 2)
        put(to_low, c * 4, acc_low, c, 2, 4)
        put(to_up, c * 4, acc_up, c, 2, 4)
        put(to_low2, c * 2, acc_low, c, 0, 2)
        put(to_up2, c * 2, acc_up, c, 6, 2)
    send_early()

    @pl.when(here >= -1)
    def _():
        backward_one(1)
        backward_one(2)

    selfs = [jnp.sum(dr[c], axis=0, keepdims=True) for c in range(3)]
    selfs = jnp.concatenate([v[:, t * 128 : (t + 1) * 128] for v in selfs for t in range(8)], 0)
    acc_own = onto(256, 512, lambda k: [lam[k * 4 + t] for t in range(4)]) - selfs
    for c in range(3):
        put(kept, c * 4, acc_own, c, 2, 4)
        put(to_low_s, c * 2, acc_own, c, 0, 2)
        put(to_up_s, c * 2, acc_own, c, 6, 2)


COMPUTE_SCRATCH = [
    pltpu.VMEM((8, 1024), I32),
    pltpu.VMEM((6, 8, 1024), F32),
    pltpu.VMEM((8, 8, 1024), F32),
    pltpu.VMEM((8, 8, 1024), F32),
    pltpu.VMEM((32, 1024, 128), BF16),
    pltpu.VMEM((9, 128, 1024), F32),
    pltpu.VMEM((8, 256, 128), BF16),
    pltpu.VMEM((128, 1024), F32),
    pltpu.VMEM((4, 8, 128, 128), F32),
    pltpu.VMEM((4, 8, 128, 128), F32),
    pltpu.VMEM((4, 9, 128, 128), F32),
    pltpu.VMEM((32, 256, 128), BF16),
    pltpu.VMEM((32, 256, 128), BF16),
    pltpu.VMEM((576, 512), F32),
    pltpu.VMEM((72, 1024), F32),
    pltpu.VMEM((128, 1024), F32),
    pltpu.VMEM((3, 8, 1024), F32),
    pltpu.VMEM((8, 1024), F32),
    pltpu.VMEM((32, 128, 128), BF16),
    pltpu.VMEM((32, 128, 128), BF16),
]


def ring_tables(beads):
    b = np.arange(beads, dtype=np.float64)
    angle = beads * np.sin(np.pi * b / beads)
    safe = np.where(b == 0, 1.0, angle)
    reach = np.where(b == 0, STEP, STEP * np.sin(angle) / safe)
    stiff = angle * np.sin(angle) / STEP
    phase = np.cos(2.0 * np.pi * np.outer(b, b) / beads) / beads
    return [(phase @ f).tolist() for f in (np.cos(angle), reach, stiff)]


def rows12(ref):
    return jnp.concatenate([ref[c, 0:1, t * 128 : (t + 1) * 128] for c in range(3) for t in range(4)], 0)


def step_kernel(
    domains, beads,
    *refs,
):
    sources, packed, held, in_sem = refs[:12], refs[12], refs[13:25], refs[25]
    (
        msg_up, msg_low, in_low, in_up, in_low2, in_up2,
        to_low, to_up, to_low2, to_up2, to_low_s, to_up_s, kept,
        from_low, from_up, from_low2, from_up2, from_low_s, from_up_s, q_src, p_src, q_all, p_all,
        fs_sem, fr_sem, hs_sem, hr_sem, qs_sem, qr_sem, ps_sem, pr_sem,
        *work,
    ) = refs[26:]
    pos, mom, spec, nbr, send_ref, emb, r1, r2, mix1, mix2, rd1, rd2 = held
    me = lax.axis_index("space")
    bead = lax.axis_index("bead")
    near = [lax.rem(me + s + domains, domains) for s in (1, -1, 2, -2)]
    ring = [lax.rem(bead + o, beads) for o in range(beads)]
    barrier = pltpu.get_barrier_semaphore()
    for p in near:
        pl.semaphore_signal(barrier, inc=1, device_id={"space": p}, device_id_type=MESH)
    for o in range(1, beads):
        pl.semaphore_signal(barrier, inc=1, device_id={"bead": ring[o]}, device_id_type=MESH)

    loads = [pltpu.make_async_copy(a, b, in_sem.at[i]) for i, (a, b) in enumerate(zip(sources, held))]
    for c in loads:
        c.start()
    for c in loads:
        c.wait()

    flags = spec[...].astype(F32)
    send = send_ref[...]
    own_t, nbr_t = [], []
    for t in range(4):
        lanes = slice(t * 128, (t + 1) * 128)
        quad = [pos[c, 0:1, lanes] for c in range(3)] + [flags[:, lanes]]
        own_t.append(jnp.concatenate(quad + quad, 0))
        nbr_t.append(nbr[:, lanes])

    def sent(tiles, half):
        return [
            lane_take(tiles, spread(send[:, at : at + 128])) for at in (half * 256, half * 256 + 128)
        ]

    def pair(x, y):
        return jnp.concatenate([x[0:4], y[4:8]], 0)

    def both(x):
        return [jnp.concatenate([x[0:4], x[0:4]], 0), jnp.concatenate([x[4:8], x[4:8]], 0)]

    ghosts = [sent(own_t, 0), sent(own_t, 1)]
    q_src[...] = rows12(pos)
    for msg, half in ((msg_low, 0), (msg_up, 1)):
        lists = sent(nbr_t, half)
        msg[0:8, :] = pair(*ghosts[half])
        msg[8:16, :] = pair(own_t[0], own_t[1])
        msg[16:24, :] = pair(own_t[2], own_t[3])
        msg[24:32, :] = lists[0].astype(F32)
        msg[32:40, :] = lists[1].astype(F32)
    pl.semaphore_wait(barrier, 4 + beads - 1)

    def to_near(first, peers, srcs, dsts, s_sem, r_sem):
        out = []
        for i, p, s, dst in zip(range(first, 6), peers, srcs, dsts):
            c = pltpu.make_async_remote_copy(
                src_ref=s, dst_ref=dst, send_sem=s_sem.at[i], recv_sem=r_sem.at[i],
                device_id={"space": p}, device_id_type=MESH,
            )
            c.start()
            out.append(c)
        return out

    def share(src, dst, s_sem, r_sem):
        out = []
        for o in range(1, beads):
            c = pltpu.make_async_remote_copy(
                src_ref=src, dst_ref=dst.at[o], send_sem=s_sem.at[o], recv_sem=r_sem.at[o],
                device_id={"bead": ring[o]}, device_id_type=MESH,
            )
            c.start()
            out.append(c)
        return out

    edge = (msg_up.at[0:8], msg_low.at[0:8])
    halo = to_near(0, near, edge, (in_low.at[0:8], in_up.at[0:8]), fs_sem, fr_sem)
    bulk = to_near(
        2, near, (msg_up.at[8:40], msg_low.at[8:40]) + edge, (in_low.at[8:40], in_up.at[8:40], in_low2, in_up2),
        fs_sem, fr_sem,
    )
    prepared = prepare(nbr, (emb, r1, r2, mix1, mix2, rd1, rd2), work)
    q_copies = share(q_src, q_all, qs_sem, qr_sem)
    for c in halo:
        c.wait()

    def whole(ref):
        return both(ref[8:16, :]) + both(ref[16:24, :])

    def rest():
        for c in bulk:
            c.wait()
        ext_low = both(in_low2[...]) + whole(in_low) + ghosts[0]
        ext_up = ghosts[1] + whole(in_up) + both(in_up2[...])
        return ext_low, ext_up, [r[a : a + 8, :].astype(I32) for r in (in_low, in_up) for a in (24, 32)]

    copies = []

    def send_early():
        copies.extend(
            to_near(0, near, (to_up, to_low, to_up2, to_low2), (from_low, from_up, from_low2, from_up2), hs_sem, hr_sem)
        )

    ext_own = both(in_low[0:8, :]) + own_t + both(in_up[0:8, :])
    energy_gradient(
        me, prepared, ext_own, nbr_t, rest, send_early,
        to_low, to_up, to_low2, to_up2, to_low_s, to_up_s, kept, *work,
    )
    copies += to_near(4, near, (to_up_s, to_low_s), (from_low_s, from_up_s), hs_sem, hr_sem)

    there = [spread(send[:, t * 128 : (t + 1) * 128] >> 7) for t in range(4)]
    iota8 = lax.broadcasted_iota(I32, (8, 128), 0)
    rhs = jnp.where(
        jnp.broadcast_to(send & 127, (128, 512)) == lax.broadcasted_iota(I32, (128, 512), 0), 1.0, 0.0
    ).astype(BF16)
    mass4 = HEAVY - (HEAVY - 1.0) * jnp.concatenate(
        [flags[:, t * 128 : (t + 1) * 128] for t in range(4)], 0
    )
    mass = jnp.concatenate([mass4, mass4, mass4], 0)
    p12 = rows12(mom)
    for c in copies:
        c.wait()

    his, los = [], []
    for c in range(3):
        parts = []
        for t in range(4):
            near_, far = (from_low_s, from_low2) if t < 2 else (from_up_s, from_up2)
            at, a2 = 12 + c * 4 + t, c * 2 + t % 2
            v = kept[at : at + 1, :] + near_[a2 : a2 + 1, :] + far[a2 : a2 + 1, :]
            parts.append(jnp.where(there[t] == iota8, spread(v), 0.0))
        m = jnp.concatenate(parts, 1)
        hi = m.astype(BF16).astype(F32)
        his.append(hi)
        los.append(m - hi)
    got = halves(dot_nt(jnp.concatenate(his + los, 0).astype(BF16), rhs))
    got = jnp.concatenate([got[c * 8 : c * 8 + 4] for c in range(3)], 0)
    kicked = p12 - (kept[0:12, :] + from_low[0:12, :] + from_up[0:12, :] + got)
    p_src[...] = kicked
    p_copies = share(p_src, p_all, ps_sem, pr_sem)

    turn, reach, stiff = ring_tables(beads)
    q = q_src[...]
    qa, qs = turn[0] * q, stiff[0] * q
    for o, c in zip(range(1, beads), q_copies):
        c.wait()
        q = q_all[o]
        qa, qs = qa + turn[o] * q, qs + stiff[o] * q
    pa, pr = turn[0] * kicked, reach[0] * kicked
    for o, c in zip(range(1, beads), p_copies):
        c.wait()
        p = p_all[o]
        pa, pr = pa + turn[o] * p, pr + reach[o] * p
    for i, v in enumerate((qa, pr / mass, pa, mass * qs)):
        for c in range(3):
            for t in range(4):
                at = c * 4 + t
                packed[i, c, 0:1, t * 128 : (t + 1) * 128] = v[at : at + 1]


def shards(
    positions, momenta, species, neighbours, send_list, embedding,
    radial_one, radial_two, mix_one, mix_two, read_one, read_two,
):
    domains, beads = lax.axis_size("space"), lax.axis_size("bead")
    dma = lambda n: pltpu.SemaphoreType.DMA((n,))
    rows = lambda n: pltpu.VMEM((n, 128), F32)
    given = (
        jnp.transpose(positions, (1, 0, 2)), jnp.transpose(momenta, (1, 0, 2)), species[None], neighbours,
        send_list[None], embedding, radial_one, radial_two, mix_one, mix_two, read_one[None], read_two[None],
    )
    out = pl.pallas_call(
        lambda *refs: step_kernel(domains, beads, *refs),
        out_shape=jax.ShapeDtypeStruct((4, 3, 1, 512), F32),
        in_specs=[pl.BlockSpec(memory_space=pl.ANY)] * 12,
        out_specs=VM,
        scratch_shapes=[pltpu.VMEM(a.shape, a.dtype) for a in given]
        + [dma(12)]
        + [rows(n) for n in (40, 40, 40, 40, 8, 8, 16, 16, 8, 8, 8, 8, 24, 16, 16, 8, 8, 8, 8, 12, 12)]
        + [pltpu.VMEM((beads, 12, 128), F32)] * 2
        + [dma(6)] * 4 + [dma(beads)] * 4 + COMPUTE_SCRATCH,
        compiler_params=pltpu.CompilerParams(
            collective_id=0, has_side_effects=True, vmem_limit_bytes=60 << 20
        ),
        name="md_step",
    )(*given)
    return jnp.transpose(out[0] + out[1], (1, 0, 2)), jnp.transpose(out[2] - out[3], (1, 0, 2))


def solution(mesh):
    beads = P("bead", None, "space")
    placed = (beads, beads, P("space"), P(None, "space"), P("space")) + (P(),) * 7
    return jax.shard_map(shards, mesh=mesh, in_specs=placed, out_specs=(beads, beads), check_vma=False)
```
